128 devices in a mesh: gx: 8 (over z, y_hi), gy: 4 (over x), gz: 4 (over y_lo, core).
Axes of the slice: x: 4, y: 4 (y_hi: 2, y_lo: 2; y = y_hi * 2 + y_lo), z: 4, core: 2. Of those that a mesh axis runs over, the one named last changes fastest.
Arguments:
- checkpoint: float32 [256, 256, 1024], P('gx', 'gy', 'gz'), may hold values from -6 to 6
- diffusivity: float32 [256, 256, 1024], P('gx', 'gy', 'gz'), may hold values from 0.1 to 1
- material_scale: float32 [4], replicated, may hold values from 0.5 to 1
- labels: int32 [256, 256, 1024], P('gx', 'gy', 'gz'), may hold values from 0 to 3
- measured: float32 [256, 256, 1024], P('gx', 'gy', 'gz'), may hold values from -6 to 6
- observed: int32 [256, 256, 1024], P('gx', 'gy', 'gz'), may hold values 0 or 1
- adjoint_in: float32 [256, 256, 1024], P('gx', 'gy', 'gz'), may hold values from -4 to 4
Outputs:
- gradient: float32 [256, 256, 1024], P('gx', 'gy', 'gz')
- adjoint_start: float32 [256, 256, 1024], P('gx', 'gy', 'gz')
The draws below stay inside these ranges and needn't reach their ends.
All inputs are finite; a program needn't handle non-finite values. No bound on the sum of `observed` on one device may be relied on, other than what follows from the above.
Results may differ from the reference program's by a relative error of at most 0.00002.
Values sent between devices are 32-bit elements; how exact they have to be, the bound alone decides.
A program may use at most 192 MiB of HBM per device.

```python
import math
import jax
import jax.numpy as jnp

ITERS = 4
MATERIALS = 4
NX = 256
NY = 256
NZ = 1024


def place_ends(values, stream_key, smallest, high):
    longest = values.shape.index(max(values.shape))
    spots = []
    for shift in (0, 1):
        where = [jax.random.randint(jax.random.fold_in(stream_key, axis), (), 0, length) for axis, length in enumerate(values.shape)]
        where[longest] = (where[longest] + shift) % values.shape[longest]
        spots.append(tuple(where))
    return values.at[spots[0]].set(smallest).at[spots[1]].set(high)


def level_of(key, dims, cuts, low, top_value):
    factor_of, own = 1.0, jax.random.fold_in(key, 6)
    for axis_at, blocks in cuts:
        heights = jnp.exp(jax.random.uniform(jax.random.fold_in(own, axis_at), (blocks,), jnp.float32, low / len(cuts), top_value / len(cuts)))
        factor_of = factor_of * jnp.repeat(heights, dims[axis_at] // blocks).reshape([-1 if axis == axis_at else 1 for axis in range(len(dims))])
    return factor_of


def noise(stream_key, shape, scale, reach, cuts=(), held_as=jnp.bfloat16):
    factor_of = level_of(stream_key, shape, cuts, -0.22, 0.18) if cuts else 1.0
    drawn = jax.random.normal(stream_key, shape, jnp.float32) * scale * factor_of
    return jnp.minimum(jnp.maximum(drawn, -reach), reach).astype(held_as)


def setup_inputs(seed: int = 0) -> dict:
    streams_of = jax.random.split(jax.random.key(seed), 8)
    return {
        "checkpoint": noise(streams_of[0], (NX, NY, NZ), 1.0, 6.0, ((0, 8), (1, 4), (2, 4)), jnp.float32),
        "diffusivity": jnp.clip(jnp.exp(math.log(1.0) - 2.3025851 * jax.random.uniform(streams_of[1], (NX, NY, NZ), jnp.float32) ** level_of(streams_of[1], (NX, NY, NZ), ((0, 8), (1, 4), (2, 4)), -0.2, 0.2)), 0.1, 1.0),
        "material_scale": jnp.clip(jax.random.uniform(streams_of[2], (MATERIALS,), jnp.float32, 0.5, 1.0), 0.5, 1.0),
        "labels": place_ends(jax.random.randint(streams_of[3], (NX, NY, NZ), 0, MATERIALS), jax.random.fold_in(streams_of[3], 1), 0, MATERIALS - 1).astype(jnp.int32),
        "measured": noise(streams_of[4], (NX, NY, NZ), 1.0, 6.0, ((0, 8), (1, 4), (2, 4)), jnp.float32),
        "observed": place_ends((jax.random.randint(streams_of[5], (NX, NY, NZ), 0, 2) < 1).astype(jnp.int32), jax.random.fold_in(streams_of[5], 1), 0, 1),
        "adjoint_in": noise(streams_of[6], (NX, NY, NZ), 0.5, 4.0, ((0, 8), (1, 4), (2, 4)), jnp.float32),
    }


RATE = 0.15


def neighbour(x, dim, off):
    parts = [slice(1, -1), slice(1, -1), slice(1, -1)]
    parts[dim] = slice(off, x.shape[dim] - 2 + off)
    return x[tuple(parts)]


def advance(field_pad, kappa_pad):
    centre = neighbour(field_pad, 0, 1)
    kcentre = neighbour(kappa_pad, 0, 1)
    total = jnp.zeros_like(centre)
    for dim in range(3):
        for off in (0, 2):
            total = total + 0.5 * (kcentre + neighbour(kappa_pad, dim, off)) * (neighbour(field_pad, dim, off) - centre)
    return centre + RATE * total


def grad_term(lam_pad, temp_pad):
    lcentre = neighbour(lam_pad, 0, 1)
    tcentre = neighbour(temp_pad, 0, 1)
    total = jnp.zeros_like(lcentre)
    for dim in range(3):
        for off in (0, 2):
            total = total + (neighbour(lam_pad, dim, off) - lcentre) * (neighbour(temp_pad, dim, off) - tcentre)
    return -0.5 * RATE * total


def reference(checkpoint, diffusivity, material_scale, labels, measured, observed, adjoint_in):
    factor = material_scale[labels]
    kappa_pad = jnp.pad(diffusivity * factor, 1)
    history = []
    temp = checkpoint
    for step in range(ITERS):
        history.append(temp)
        temp = advance(jnp.pad(temp, 1), kappa_pad)
    lam = adjoint_in + observed.astype(jnp.float32) * (temp - measured)
    acc = jnp.zeros_like(checkpoint)
    for step in range(ITERS - 1, -1, -1):
        lam_pad = jnp.pad(lam, 1)
        acc = acc + grad_term(lam_pad, jnp.pad(history[step], 1))
        lam = advance(lam_pad, kappa_pad)
    return acc * factor, lam
```

```python
import functools

import jax
import jax.numpy as jnp
from jax import lax
from jax.experimental import pallas as pl
from jax.experimental.pallas import tpu as pltpu
from jax.sharding import PartitionSpec as P

ITERS = 4
MATERIALS = 4

RATE = 0.15
HALF_RATE = 0.5 * RATE
AXES = ("gx", "gy", "gz")
LANES = 128
VMEM_LIMIT = 56 * 1024 * 1024
MESH_ID = pl.DeviceIdType.MESH


def _vmem():
    return pl.BlockSpec(memory_space=pltpu.VMEM)


def _smem():
    return pl.BlockSpec(memory_space=pltpu.SMEM)


class Geo:
    def __init__(self, shape):
        self.X, self.Y, self.Z = shape
        self.row = lax.broadcasted_iota(jnp.int32, (self.Y, self.Z), 0)
        self.lane = lax.broadcasted_iota(jnp.int32, (self.Y, self.Z), 1)
        self.lane128 = lax.broadcasted_iota(jnp.int32, (self.Y, LANES), 1)

    def widen(self, v):
        return jnp.concatenate([v] * (self.Z // LANES), axis=1)


def _slab_nbrs(g, F, halo, x, pos):
    xh, yh, zh = halo
    c = F[x]
    xm = xh[0] if pos == "first" else F[x - 1]
    xp = xh[1] if pos == "last" else F[x + 1]
    ym = jnp.where(g.row == 0, yh[0, pl.ds(x, 1), :], pltpu.roll(c, 1, 0))
    yp = jnp.where(g.row == g.Y - 1, yh[1, pl.ds(x, 1), :], pltpu.roll(c, g.Y - 1, 0))
    zlo = pltpu.roll(zh[0], lax.rem(LANES - x, LANES), 1)
    zhi = pltpu.roll(zh[1], lax.rem(LANES - 1 - x + LANES, LANES), 1)
    zm = jnp.where(g.lane == 0, g.widen(zlo), pltpu.roll(c, 1, 1))
    zp = jnp.where(g.lane == g.Z - 1, g.widen(zhi), pltpu.roll(c, g.Z - 1, 1))
    return c, (xm, xp, ym, yp, zm, zp)


def _pack(g, faces, x, new, pos):
    xs, ys, zs = faces
    if pos == "first":
        xs[0] = new
    if pos == "last":
        xs[1] = new
    ys[0, pl.ds(x, 1), :] = new[0:1, :]
    ys[1, pl.ds(x, 1), :] = new[g.Y - 1 : g.Y, :]
    w0 = pltpu.roll(new[:, 0:LANES], x, 1)
    w1 = pltpu.roll(new[:, g.Z - LANES : g.Z], lax.rem(x + 1, LANES), 1)
    zs[0] = jnp.where(g.lane128 == x, w0, zs[0])
    zs[1] = jnp.where(g.lane128 == x, w1, zs[1])


def _zero_faces(faces):
    zs = faces[2]
    zs[...] = jnp.zeros(zs.shape, zs.dtype)


def _over_slabs(X, body):
    body(0, "first")
    if X > 2:

        def step(x, carry):
            body(x, "mid")
            return carry

        lax.fori_loop(1, X - 1, step, 0)
    body(X - 1, "last")


def _factor(scale, lab):
    f = jnp.where(lab == 2, scale[2], scale[3])
    f = jnp.where(lab == 1, scale[1], f)
    return jnp.where(lab == 0, scale[0], f)


def _stencil(c, nb, kc, knb):
    total = jnp.zeros_like(c)
    for v, k in zip(nb, knb):
        total = total + (kc + k) * (v - c)
    return c + HALF_RATE * total


def _prep_kernel(diff, labels, scale, ckpt, kap, xs, ys, zs):
    g = Geo(diff.shape)
    kf = (xs.at[0], ys.at[0], zs.at[0])
    uf = (xs.at[1], ys.at[1], zs.at[1])
    _zero_faces((xs, ys, zs))

    def body(x, pos):
        k = diff[x] * _factor(scale, labels[x])
        kap[x] = k
        _pack(g, kf, x, k, pos)
        _pack(g, uf, x, ckpt[x], pos)

    _over_slabs(g.X, body)


def _fwd_kernel(last, u, uxh, uyh, uzh, kap, kxh, kyh, kzh, *rest):
    if last:
        adj, obs, meas, out, xs, ys, zs = rest
    else:
        out, xs, ys, zs = rest
    g = Geo(u.shape)
    faces = (xs, ys, zs)
    _zero_faces(faces)

    def body(x, pos):
        c, nb = _slab_nbrs(g, u, (uxh, uyh, uzh), x, pos)
        kc, knb = _slab_nbrs(g, kap, (kxh, kyh, kzh), x, pos)
        new = _stencil(c, nb, kc, knb)
        if last:
            new = adj[x] + obs[x].astype(jnp.float32) * (new - meas[x])
        out[x] = new
        _pack(g, faces, x, new, pos)

    _over_slabs(g.X, body)


def _bwd_kernel(first, final, lam, lxh, lyh, lzh, u, uxh, uyh, uzh, kap, kxh, kyh, kzh, *rest):
    rest = list(rest)
    acc_in = None if first else rest.pop(0)
    if final:
        labels, scale, lam_out, acc_out = rest
        faces = None
    else:
        lam_out, acc_out, xs, ys, zs = rest
        faces = (xs, ys, zs)
        _zero_faces(faces)
    g = Geo(lam.shape)

    def body(x, pos):
        lc, lnb = _slab_nbrs(g, lam, (lxh, lyh, lzh), x, pos)
        uc, unb = _slab_nbrs(g, u, (uxh, uyh, uzh), x, pos)
        kc, knb = _slab_nbrs(g, kap, (kxh, kyh, kzh), x, pos)
        s = jnp.zeros_like(lc)
        t = jnp.zeros_like(lc)
        for lj, uj, kj in zip(lnb, unb, knb):
            d = lj - lc
            s = s + (kc + kj) * d
            t = t + d * (uj - uc)
        new = lc + HALF_RATE * s
        term = (-HALF_RATE) * t
        acc = term if first else acc_in[x] + term
        if final:
            acc = acc * _factor(scale, labels[x])
        acc_out[x] = acc
        lam_out[x] = new
        if faces is not None:
            _pack(g, faces, x, new, pos)

    _over_slabs(g.X, body)


def _comm_kernel(sizes, xs, ys, zs, xh, yh, zh, send_sem, recv_sem):
    nf = xs.shape[0]
    idx = [lax.axis_index(a) for a in AXES]

    def nbr(a, d):
        coords = list(idx)
        coords[a] = idx[a] + d
        return tuple(coords)

    def has(a, d):
        return jnp.logical_and(idx[a] + d >= 0, idx[a] + d < sizes[a])

    barrier = pltpu.get_barrier_semaphore()
    count = jnp.int32(0)
    for a in range(3):
        for d in (-1, 1):

            @pl.when(has(a, d))
            def _():
                pl.semaphore_signal(barrier, 1, device_id=nbr(a, d), device_id_type=MESH_ID)

            count = count + has(a, d).astype(jnp.int32)
    pl.semaphore_wait(barrier, count)

    bufs = ((xs, xh), (ys, yh), (zs, zh))
    for a, (_, dst) in enumerate(bufs):
        for s, d in ((0, -1), (1, 1)):

            @pl.when(jnp.logical_not(has(a, d)))
            def _():
                dst[:, s] = jnp.zeros(dst.shape[:1] + dst.shape[2:], dst.dtype)

    def copy(f, a, s):
        src, dst = bufs[a]
        k = 2 * a + s
        d = 1 if s == 0 else -1
        return pltpu.make_async_remote_copy(
            src_ref=src.at[f, 1 - s],
            dst_ref=dst.at[f, s],
            send_sem=send_sem.at[f, k],
            recv_sem=recv_sem.at[f, k],
            device_id=nbr(a, d),
            device_id_type=MESH_ID,
        )

    for f in range(nf):
        for a in range(3):
            for s in (0, 1):
                d = 1 if s == 0 else -1

                @pl.when(has(a, d))
                def _():
                    copy(f, a, s).start()

    for f in range(nf):
        for a in range(3):
            for s in (0, 1):
                d_send = 1 if s == 0 else -1
                d_recv = -1 if s == 0 else 1

                @pl.when(has(a, d_recv))
                def _():
                    copy(f, a, s).wait_recv()

                @pl.when(has(a, d_send))
                def _():
                    copy(f, a, s).wait_send()


def _face_shapes(shape, nf=None):
    X, Y, Z = shape
    lead = (2,) if nf is None else (nf, 2)
    return (
        jax.ShapeDtypeStruct(lead + (Y, Z), jnp.float32),
        jax.ShapeDtypeStruct(lead + (X, Z), jnp.float32),
        jax.ShapeDtypeStruct(lead + (Y, LANES), jnp.float32),
    )


def _params(**kw):
    return pltpu.CompilerParams(vmem_limit_bytes=VMEM_LIMIT, **kw)


def _call(kernel, n_in, out_shape, smem_at=(), **kw):
    in_specs = [_smem() if i in smem_at else _vmem() for i in range(n_in)]
    return pl.pallas_call(
        kernel,
        out_shape=out_shape,
        in_specs=in_specs,
        out_specs=tuple(_vmem() for _ in out_shape),
        compiler_params=_params(**kw),
    )


def _exchange(sizes, faces):
    xs, ys, zs = faces
    nf = xs.shape[0]
    out_shape = (
        jax.ShapeDtypeStruct(xs.shape, xs.dtype),
        jax.ShapeDtypeStruct(ys.shape, ys.dtype),
        jax.ShapeDtypeStruct(zs.shape, zs.dtype),
    )
    return pl.pallas_call(
        functools.partial(_comm_kernel, sizes),
        out_shape=out_shape,
        in_specs=[_vmem()] * 3,
        out_specs=tuple(_vmem() for _ in out_shape),
        scratch_shapes=[pltpu.SemaphoreType.DMA((nf, 6)), pltpu.SemaphoreType.DMA((nf, 6))],
        compiler_params=_params(collective_id=nf - 1, has_side_effects=True),
    )(xs, ys, zs)


def _pick(h, f):
    return tuple(a[f] for a in h)


def _shards(sizes, checkpoint, diffusivity, material_scale, labels, measured, observed, adjoint_in):
    shape = checkpoint.shape
    field = jax.ShapeDtypeStruct(shape, jnp.float32)

    kap, xs, ys, zs = _call(_prep_kernel, 4, (field,) + _face_shapes(shape, 2), smem_at=(2,))(
        diffusivity, labels, material_scale, checkpoint
    )
    h = _exchange(sizes, (xs, ys, zs))
    kh = _pick(h, 0)
    uh = [_pick(h, 1)]
    us = [checkpoint]

    for n in range(ITERS):
        last = n == ITERS - 1
        extra = (adjoint_in, observed, measured) if last else ()
        new, xs, ys, zs = _call(
            functools.partial(_fwd_kernel, last), 8 + len(extra), (field,) + _face_shapes(shape)
        )(us[n], *uh[n], kap, *kh, *extra)
        h = _exchange(sizes, (xs[None], ys[None], zs[None]))
        if last:
            lam, lh = new, _pick(h, 0)
        else:
            us.append(new)
            uh.append(_pick(h, 0))

    acc = None
    for n in range(ITERS - 1, -1, -1):
        first = n == ITERS - 1
        final = n == 0
        ins = [lam, *lh, us[n], *uh[n], kap, *kh]
        if not first:
            ins.append(acc)
        if final:
            ins += [labels, material_scale]
            outs = (field, field)
            smem_at = (len(ins) - 1,)
        else:
            outs = (field, field) + _face_shapes(shape)
            smem_at = ()
        res = _call(functools.partial(_bwd_kernel, first, final), len(ins), outs, smem_at=smem_at)(*ins)
        if final:
            lam, acc = res
        else:
            lam, acc, xs, ys, zs = res
            h = _exchange(sizes, (xs[None], ys[None], zs[None]))
            lh = _pick(h, 0)
    return acc, lam


def solution(mesh):
    sizes = tuple(mesh.shape[a] for a in AXES)
    block = P("gx", "gy", "gz")
    placed = (block, block, P(), block, block, block, block)
    return jax.shard_map(
        functools.partial(_shards, sizes),
        mesh=mesh,
        in_specs=placed,
        out_specs=(block, block),
        check_vma=False,
    )
```

```python
import functools

import jax
import jax.numpy as jnp
from jax import lax
from jax.experimental import pallas as pl
from jax.experimental.pallas import tpu as pltpu
from jax.sharding import PartitionSpec as P

ITERS = 4
MATERIALS = 4

RATE = 0.15
HALF_RATE = 0.5 * RATE
AXES = ("gx", "gy", "gz")
LANES = 128
VMEM_LIMIT = 56 * 1024 * 1024
MESH_ID = pl.DeviceIdType.MESH


def _vmem():
    return pl.BlockSpec(memory_space=pltpu.VMEM)


def _smem():
    return pl.BlockSpec(memory_space=pltpu.SMEM)


class Geo:
    def __init__(self, shape):
        self.X, self.Y, self.Z = shape
        self.row = lax.broadcasted_iota(jnp.int32, (self.Y, self.Z), 0)
        self.lane = lax.broadcasted_iota(jnp.int32, (self.Y, self.Z), 1)
        self.lane128 = lax.broadcasted_iota(jnp.int32, (self.Y, LANES), 1)

    def widen(self, v):
        return jnp.concatenate([v] * (self.Z // LANES), axis=1)


def _slab_nbrs(g, F, halo, x, pos):
    xh, yh, zh = halo
    c = F[x]
    xm = xh[0] if pos == "first" else F[x - 1]
    xp = xh[1] if pos == "last" else F[x + 1]
    ym = jnp.where(g.row == 0, yh[0, pl.ds(x, 1), :], pltpu.roll(c, 1, 0))
    yp = jnp.where(g.row == g.Y - 1, yh[1, pl.ds(x, 1), :], pltpu.roll(c, g.Y - 1, 0))
    zlo = pltpu.roll(zh[0], lax.rem(LANES - x, LANES), 1)
    zhi = pltpu.roll(zh[1], lax.rem(LANES - 1 - x + LANES, LANES), 1)
    zm = jnp.where(g.lane == 0, g.widen(zlo), pltpu.roll(c, 1, 1))
    zp = jnp.where(g.lane == g.Z - 1, g.widen(zhi), pltpu.roll(c, g.Z - 1, 1))
    return c, (xm, xp, ym, yp, zm, zp)


def _pack(g, faces, x, new, pos):
    xs, ys, zs = faces
    if pos == "first":
        xs[0] = new
    if pos == "last":
        xs[1] = new
    ys[0, pl.ds(x, 1), :] = new[0:1, :]
    ys[1, pl.ds(x, 1), :] = new[g.Y - 1 : g.Y, :]
    w0 = pltpu.roll(new[:, 0:LANES], x, 1)
    w1 = pltpu.roll(new[:, g.Z - LANES : g.Z], lax.rem(x + 1, LANES), 1)
    zs[0] = jnp.where(g.lane128 == x, w0, zs[0])
    zs[1] = jnp.where(g.lane128 == x, w1, zs[1])


def _zero_faces(faces):
    zs = faces[2]
    zs[...] = jnp.zeros(zs.shape, zs.dtype)


def _over_slabs(X, body):
    body(0, "first")
    if X > 2:

        def step(x, carry):
            body(x, "mid")
            return carry

        lax.fori_loop(1, X - 1, step, 0)
    body(X - 1, "last")


def _factor(scale, lab):
    f = jnp.where(lab == 2, scale[2], scale[3])
    f = jnp.where(lab == 1, scale[1], f)
    return jnp.where(lab == 0, scale[0], f)


def _stencil(c, nb, kc, knb):
    total = jnp.zeros_like(c)
    for v, k in zip(nb, knb):
        total = total + (kc + k) * (v - c)
    return c + HALF_RATE * total


N_EX = 2 * ITERS + 1


def _window_kernel(
    sizes,
    ckpt, diff, scale, labels, meas, obs, adj,
    grad, lam_out,
    kap, u1, u2, u3, la, lb, xs, ys, zs, xh, yh, zh, send_sem, recv_sem,
):
    g = Geo(ckpt.shape)
    idx = [lax.axis_index(a) for a in AXES]

    def nbr(a, d):
        coords = list(idx)
        coords[a] = idx[a] + d
        return tuple(coords)

    def has(a, d):
        return jnp.logical_and(idx[a] + d >= 0, idx[a] + d < sizes[a])

    zs[...] = jnp.zeros(zs.shape, zs.dtype)
    halos = (xh, yh, zh)
    for a, dst in enumerate(halos):
        for s, d in ((0, -1), (1, 1)):

            @pl.when(jnp.logical_not(has(a, d)))
            def _():
                dst[:, s] = jnp.zeros(dst.shape[:1] + dst.shape[2:], dst.dtype)

    barrier = pltpu.get_barrier_semaphore()
    count = jnp.int32(0)
    for a in range(3):
        for d in (-1, 1):

            @pl.when(has(a, d))
            def _():
                pl.semaphore_signal(barrier, 1, device_id=nbr(a, d), device_id_type=MESH_ID)

            count = count + has(a, d).astype(jnp.int32)
    pl.semaphore_wait(barrier, count)

    sends = (xs, ys, zs)

    def copy(e, a, s):
        k = 2 * a + s
        return pltpu.make_async_remote_copy(
            src_ref=sends[a].at[e, 1 - s],
            dst_ref=halos[a].at[e, s],
            send_sem=send_sem.at[e, k],
            recv_sem=recv_sem.at[e, k],
            device_id=nbr(a, 1 if s == 0 else -1),
            device_id_type=MESH_ID,
        )

    def start(e):
        for a in range(3):
            for s in (0, 1):

                @pl.when(has(a, 1 if s == 0 else -1))
                def _():
                    copy(e, a, s).start()

    def wait(e):
        for a in range(3):
            for s in (0, 1):

                @pl.when(has(a, -1 if s == 0 else 1))
                def _():
                    copy(e, a, s).wait_recv()

                @pl.when(has(a, 1 if s == 0 else -1))
                def _():
                    copy(e, a, s).wait_send()

    def faces(e):
        return (xs.at[e], ys.at[e], zs.at[e])

    def halo(e):
        return (xh.at[e], yh.at[e], zh.at[e])

    def prep(x, pos):
        k = diff[x] * _factor(scale, labels[x])
        kap[x] = k
        _pack(g, faces(0), x, k, pos)
        _pack(g, faces(1), x, ckpt[x], pos)

    _over_slabs(g.X, prep)
    start(0)
    start(1)
    wait(0)
    wait(1)
    kh = halo(0)

    us = (ckpt, u1, u2, u3)
    for n in range(ITERS):
        last = n == ITERS - 1
        src, out = us[n], (la if last else us[n + 1])
        e_in, e_out = 1 + n, 2 + n

        def fwd(x, pos):
            c, nb = _slab_nbrs(g, src, halo(e_in), x, pos)
            kc, knb = _slab_nbrs(g, kap, kh, x, pos)
            new = _stencil(c, nb, kc, knb)
            if last:
                new = adj[x] + obs[x].astype(jnp.float32) * (new - meas[x])
            out[x] = new
            _pack(g, faces(e_out), x, new, pos)

        _over_slabs(g.X, fwd)
        start(e_out)
        wait(e_out)

    lams = (la, lb, la, lb)
    for i, n in enumerate(range(ITERS - 1, -1, -1)):
        first, final = n == ITERS - 1, n == 0
        lam, u = lams[i], us[n]
        e_lam, e_u, e_out = ITERS + 1 + i, 1 + n, ITERS + 2 + i
        out = lam_out if final else lams[i + 1]

        def bwd(x, pos):
            lc, lnb = _slab_nbrs(g, lam, halo(e_lam), x, pos)
            uc, unb = _slab_nbrs(g, u, halo(e_u), x, pos)
            kc, knb = _slab_nbrs(g, kap, kh, x, pos)
            s = jnp.zeros_like(lc)
            t = jnp.zeros_like(lc)
            for lj, uj, kj in zip(lnb, unb, knb):
                d = lj - lc
                s = s + (kc + kj) * d
                t = t + d * (uj - uc)
            new = lc + HALF_RATE * s
            term = (-HALF_RATE) * t
            acc = term if first else grad[x] + term
            if final:
                acc = acc * _factor(scale, labels[x])
            grad[x] = acc
            out[x] = new
            if not final:
                _pack(g, faces(e_out), x, new, pos)

        _over_slabs(g.X, bwd)
        if not final:
            start(e_out)
            wait(e_out)


def _shards(sizes, checkpoint, diffusivity, material_scale, labels, measured, observed, adjoint_in):
    X, Y, Z = checkpoint.shape
    field = jax.ShapeDtypeStruct((X, Y, Z), jnp.float32)
    f32 = jnp.float32
    in_specs = [_vmem(), _vmem(), _smem(), _vmem(), _vmem(), _vmem(), _vmem()]
    return pl.pallas_call(
        functools.partial(_window_kernel, sizes),
        out_shape=(field, field),
        in_specs=in_specs,
        out_specs=(_vmem(), _vmem()),
        scratch_shapes=[pltpu.VMEM((X, Y, Z), f32) for _ in range(6)]
        + [
            pltpu.VMEM((N_EX, 2, Y, Z), f32),
            pltpu.VMEM((N_EX, 2, X, Z), f32),
            pltpu.VMEM((N_EX, 2, Y, LANES), f32),
            pltpu.VMEM((N_EX, 2, Y, Z), f32),
            pltpu.VMEM((N_EX, 2, X, Z), f32),
            pltpu.VMEM((N_EX, 2, Y, LANES), f32),
            pltpu.SemaphoreType.DMA((N_EX, 6)),
            pltpu.SemaphoreType.DMA((N_EX, 6)),
        ],
        compiler_params=pltpu.CompilerParams(
            vmem_limit_bytes=VMEM_LIMIT, collective_id=0, has_side_effects=True
        ),
    )(checkpoint, diffusivity, material_scale, labels, measured, observed, adjoint_in)


def solution(mesh):
    sizes = tuple(mesh.shape[a] for a in AXES)
    block = P("gx", "gy", "gz")
    placed = (block, block, P(), block, block, block, block)
    return jax.shard_map(
        functools.partial(_shards, sizes),
        mesh=mesh,
        in_specs=placed,
        out_specs=(block, block),
        check_vma=False,
    )
```

```python
import functools

import jax
import jax.numpy as jnp
from jax import lax
from jax.experimental import pallas as pl
from jax.experimental.pallas import tpu as pltpu
from jax.sharding import PartitionSpec as P

ITERS = 4
MATERIALS = 4

RATE = 0.15
HALF_RATE = 0.5 * RATE
AXES = ("gx", "gy", "gz")
LANES = 128
VMEM_LIMIT = 56 * 1024 * 1024
MESH_ID = pl.DeviceIdType.MESH


def _vmem():
    return pl.BlockSpec(memory_space=pltpu.VMEM)


def _smem():
    return pl.BlockSpec(memory_space=pltpu.SMEM)


class Geo:
    def __init__(self, shape):
        self.X, self.Y, self.Z = shape
        self.row = lax.broadcasted_iota(jnp.int32, (self.Y, self.Z), 0)
        self.lane = lax.broadcasted_iota(jnp.int32, (self.Y, self.Z), 1)
        self.lane128 = lax.broadcasted_iota(jnp.int32, (self.Y, LANES), 1)
        self.row8 = lax.broadcasted_iota(jnp.int32, (8, self.Z), 0)

    def widen(self, v):
        return jnp.concatenate([v] * (self.Z // LANES), axis=1)


def _slab_nbrs(g, F, halo, x, pos):
    xh, yh, zh = halo
    Y, Z = g.Y, g.Z
    c = F[x]
    xm = xh[0] if pos == "first" else F[x - 1]
    xp = xh[1] if pos == "last" else F[x + 1]
    ym = pltpu.roll(c, 1, 0)
    ym = jnp.concatenate([jnp.where(g.row8 == 0, yh[0, pl.ds(x, 1), :], ym[0:8]), ym[8:]], axis=0)
    yp = pltpu.roll(c, Y - 1, 0)
    yp = jnp.concatenate([yp[: Y - 8], jnp.where(g.row8 == 7, yh[1, pl.ds(x, 1), :], yp[Y - 8 :])], axis=0)
    zlo = pltpu.roll(zh[0], lax.rem(LANES - x, LANES), 1)
    zhi = pltpu.roll(zh[1], lax.rem(LANES - 1 - x + LANES, LANES), 1)
    zm = pltpu.roll(c, 1, 1)
    zm = jnp.concatenate([jnp.where(g.lane128 == 0, zlo, zm[:, 0:LANES]), zm[:, LANES:]], axis=1)
    zp = pltpu.roll(c, Z - 1, 1)
    zp = jnp.concatenate(
        [zp[:, : Z - LANES], jnp.where(g.lane128 == LANES - 1, zhi, zp[:, Z - LANES :])], axis=1
    )
    return c, (xm, xp, ym, yp, zm, zp)


def _pack(g, faces, x, new, pos):
    xs, ys, zs = faces
    if pos == "first":
        xs[0] = new
    if pos == "last":
        xs[1] = new
    ys[0, pl.ds(x, 1), :] = new[0:1, :]
    ys[1, pl.ds(x, 1), :] = new[g.Y - 1 : g.Y, :]
    w0 = pltpu.roll(new[:, 0:LANES], x, 1)
    w1 = pltpu.roll(new[:, g.Z - LANES : g.Z], lax.rem(x + 1, LANES), 1)
    zs[0] = jnp.where(g.lane128 == x, w0, zs[0])
    zs[1] = jnp.where(g.lane128 == x, w1, zs[1])


def _zero_faces(faces):
    zs = faces[2]
    zs[...] = jnp.zeros(zs.shape, zs.dtype)


def _over_slabs(X, body):
    body(0, "first")
    if X > 2:

        def step(x, carry):
            body(x, "mid")
            return carry

        lax.fori_loop(1, X - 1, step, 0)
    body(X - 1, "last")


def _factor(scale, lab):
    f = jnp.where(lab == 2, scale[2], scale[3])
    f = jnp.where(lab == 1, scale[1], f)
    return jnp.where(lab == 0, scale[0], f)


def _stencil(c, nb, conds):
    total = jnp.zeros_like(c)
    for v, k in zip(nb, conds):
        total = total + k * (v - c)
    return c + HALF_RATE * total


N_EX = 2 * ITERS + 1


def _window_kernel(
    sizes,
    ckpt, diff, scale, labels, meas, obs, adj,
    grad, lam_out,
    kap, cond, u1, u2, u3, la, lb, xs, ys, zs, xh, yh, zh, send_sem, recv_sem,
):
    g = Geo(ckpt.shape)
    idx = [lax.axis_index(a) for a in AXES]

    def nbr(a, d):
        coords = list(idx)
        coords[a] = idx[a] + d
        return tuple(coords)

    def has(a, d):
        return jnp.logical_and(idx[a] + d >= 0, idx[a] + d < sizes[a])

    zs[...] = jnp.zeros(zs.shape, zs.dtype)
    halos = (xh, yh, zh)
    for a, dst in enumerate(halos):
        for s, d in ((0, -1), (1, 1)):

            @pl.when(jnp.logical_not(has(a, d)))
            def _():
                dst[:, s] = jnp.zeros(dst.shape[:1] + dst.shape[2:], dst.dtype)

    barrier = pltpu.get_barrier_semaphore()
    count = jnp.int32(0)
    for a in range(3):
        for d in (-1, 1):

            @pl.when(has(a, d))
            def _():
                pl.semaphore_signal(barrier, 1, device_id=nbr(a, d), device_id_type=MESH_ID)

            count = count + has(a, d).astype(jnp.int32)
    pl.semaphore_wait(barrier, count)

    sends = (xs, ys, zs)

    def copy(e, a, s):
        k = 2 * a + s
        return pltpu.make_async_remote_copy(
            src_ref=sends[a].at[e, 1 - s],
            dst_ref=halos[a].at[e, s],
            send_sem=send_sem.at[e, k],
            recv_sem=recv_sem.at[e, k],
            device_id=nbr(a, 1 if s == 0 else -1),
            device_id_type=MESH_ID,
        )

    def start(e):
        for a in range(3):
            for s in (0, 1):

                @pl.when(has(a, 1 if s == 0 else -1))
                def _():
                    copy(e, a, s).start()

    def wait(e):
        for a in range(3):
            for s in (0, 1):

                @pl.when(has(a, -1 if s == 0 else 1))
                def _():
                    copy(e, a, s).wait_recv()

                @pl.when(has(a, 1 if s == 0 else -1))
                def _():
                    copy(e, a, s).wait_send()

    def faces(e):
        return (xs.at[e], ys.at[e], zs.at[e])

    def halo(e):
        return (xh.at[e], yh.at[e], zh.at[e])

    def prep(x, pos):
        k = diff[x] * _factor(scale, labels[x])
        kap[x] = k
        _pack(g, faces(0), x, k, pos)
        _pack(g, faces(1), x, ckpt[x], pos)

    _over_slabs(g.X, prep)
    start(0)
    start(1)
    wait(0)

    def conduct(x, pos):
        kc, knb = _slab_nbrs(g, kap, halo(0), x, pos)
        for j, kj in enumerate(knb):
            cond[j, x] = kc + kj

    _over_slabs(g.X, conduct)
    wait(1)

    us = (ckpt, u1, u2, u3)
    for n in range(ITERS):
        last = n == ITERS - 1
        src, out = us[n], (la if last else us[n + 1])
        e_in, e_out = 1 + n, 2 + n

        def fwd(x, pos):
            c, nb = _slab_nbrs(g, src, halo(e_in), x, pos)
            new = _stencil(c, nb, [cond[j, x] for j in range(6)])
            if last:
                new = adj[x] + obs[x].astype(jnp.float32) * (new - meas[x])
            out[x] = new
            _pack(g, faces(e_out), x, new, pos)

        _over_slabs(g.X, fwd)
        start(e_out)
        wait(e_out)

    lams = (la, lb, la, lb)
    for i, n in enumerate(range(ITERS - 1, -1, -1)):
        first, final = n == ITERS - 1, n == 0
        lam, u = lams[i], us[n]
        e_lam, e_u, e_out = ITERS + 1 + i, 1 + n, ITERS + 2 + i
        out = lam_out if final else lams[i + 1]

        def bwd(x, pos):
            lc, lnb = _slab_nbrs(g, lam, halo(e_lam), x, pos)
            uc, unb = _slab_nbrs(g, u, halo(e_u), x, pos)
            s = jnp.zeros_like(lc)
            t = jnp.zeros_like(lc)
            for j, (lj, uj) in enumerate(zip(lnb, unb)):
                d = lj - lc
                s = s + cond[j, x] * d
                t = t + d * (uj - uc)
            new = lc + HALF_RATE * s
            term = (-HALF_RATE) * t
            acc = term if first else grad[x] + term
            if final:
                acc = acc * _factor(scale, labels[x])
            grad[x] = acc
            out[x] = new
            if not final:
                _pack(g, faces(e_out), x, new, pos)

        _over_slabs(g.X, bwd)
        if not final:
            start(e_out)
            wait(e_out)


def _shards(sizes, checkpoint, diffusivity, material_scale, labels, measured, observed, adjoint_in):
    X, Y, Z = checkpoint.shape
    field = jax.ShapeDtypeStruct((X, Y, Z), jnp.float32)
    f32 = jnp.float32
    in_specs = [_vmem(), _vmem(), _smem(), _vmem(), _vmem(), _vmem(), _vmem()]
    return pl.pallas_call(
        functools.partial(_window_kernel, sizes),
        out_shape=(field, field),
        in_specs=in_specs,
        out_specs=(_vmem(), _vmem()),
        scratch_shapes=[pltpu.VMEM((X, Y, Z), f32), pltpu.VMEM((6, X, Y, Z), f32)]
        + [pltpu.VMEM((X, Y, Z), f32) for _ in range(5)]
        + [
            pltpu.VMEM((N_EX, 2, Y, Z), f32),
            pltpu.VMEM((N_EX, 2, X, Z), f32),
            pltpu.VMEM((N_EX, 2, Y, LANES), f32),
            pltpu.VMEM((N_EX, 2, Y, Z), f32),
            pltpu.VMEM((N_EX, 2, X, Z), f32),
            pltpu.VMEM((N_EX, 2, Y, LANES), f32),
            pltpu.SemaphoreType.DMA((N_EX, 6)),
            pltpu.SemaphoreType.DMA((N_EX, 6)),
        ],
        compiler_params=pltpu.CompilerParams(
            vmem_limit_bytes=VMEM_LIMIT, collective_id=0, has_side_effects=True
        ),
    )(checkpoint, diffusivity, material_scale, labels, measured, observed, adjoint_in)


def solution(mesh):
    sizes = tuple(mesh.shape[a] for a in AXES)
    block = P("gx", "gy", "gz")
    placed = (block, block, P(), block, block, block, block)
    return jax.shard_map(
        functools.partial(_shards, sizes),
        mesh=mesh,
        in_specs=placed,
        out_specs=(block, block),
        check_vma=False,
    )
```

```python
import functools

import jax
import jax.numpy as jnp
from jax import lax
from jax.experimental import pallas as pl
from jax.experimental.pallas import tpu as pltpu
from jax.sharding import PartitionSpec as P

ITERS = 4
MATERIALS = 4

RATE = 0.15
HALF_RATE = 0.5 * RATE
AXES = ("gx", "gy", "gz")
LANES = 128
VMEM_LIMIT = 56 * 1024 * 1024
MESH_ID = pl.DeviceIdType.MESH


def _vmem():
    return pl.BlockSpec(memory_space=pltpu.VMEM)


def _smem():
    return pl.BlockSpec(memory_space=pltpu.SMEM)


class Geo:
    def __init__(self, shape):
        self.X, self.Y, self.Z = shape
        self.row = lax.broadcasted_iota(jnp.int32, (self.Y, self.Z), 0)
        self.lane = lax.broadcasted_iota(jnp.int32, (self.Y, self.Z), 1)
        self.lane128 = lax.broadcasted_iota(jnp.int32, (self.Y, LANES), 1)
        self.row8 = lax.broadcasted_iota(jnp.int32, (8, self.Z), 0)

    def widen(self, v):
        return jnp.concatenate([v] * (self.Z // LANES), axis=1)


def _slab_nbrs(g, F, halo, x, pos):
    xh, yh, zh = halo
    Y, Z = g.Y, g.Z
    c = F[x]
    xm = xh[0] if pos == "first" else F[x - 1]
    xp = xh[1] if pos == "last" else F[x + 1]
    ym = pltpu.roll(c, 1, 0)
    ym = jnp.concatenate([jnp.where(g.row8 == 0, yh[0, pl.ds(x, 1), :], ym[0:8]), ym[8:]], axis=0)
    yp = pltpu.roll(c, Y - 1, 0)
    yp = jnp.concatenate([yp[: Y - 8], jnp.where(g.row8 == 7, yh[1, pl.ds(x, 1), :], yp[Y - 8 :])], axis=0)
    zlo = pltpu.roll(zh[0], lax.rem(LANES - x, LANES), 1)
    zhi = pltpu.roll(zh[1], lax.rem(LANES - 1 - x + LANES, LANES), 1)
    zm = pltpu.roll(c, 1, 1)
    zm = jnp.concatenate([jnp.where(g.lane128 == 0, zlo, zm[:, 0:LANES]), zm[:, LANES:]], axis=1)
    zp = pltpu.roll(c, Z - 1, 1)
    zp = jnp.concatenate(
        [zp[:, : Z - LANES], jnp.where(g.lane128 == LANES - 1, zhi, zp[:, Z - LANES :])], axis=1
    )
    return c, (xm, xp, ym, yp, zm, zp)


def _local_nbrs(g, F, x, pos):
    Y, Z = g.Y, g.Z
    c = F[x]
    xm = c if pos == "first" else F[x - 1]
    xp = c if pos == "last" else F[x + 1]
    ym = pltpu.roll(c, 1, 0)
    ym = jnp.concatenate([jnp.where(g.row8 == 0, c[0:8], ym[0:8]), ym[8:]], axis=0)
    yp = pltpu.roll(c, Y - 1, 0)
    yp = jnp.concatenate([yp[: Y - 8], jnp.where(g.row8 == 7, c[Y - 8 :], yp[Y - 8 :])], axis=0)
    zm = pltpu.roll(c, 1, 1)
    zm = jnp.concatenate([jnp.where(g.lane128 == 0, c[:, 0:LANES], zm[:, 0:LANES]), zm[:, LANES:]], axis=1)
    zp = pltpu.roll(c, Z - 1, 1)
    zp = jnp.concatenate(
        [zp[:, : Z - LANES], jnp.where(g.lane128 == LANES - 1, c[:, Z - LANES :], zp[:, Z - LANES :])],
        axis=1,
    )
    return c, (xm, xp, ym, yp, zm, zp)


def _edges(g, halo, x, pos):
    xh, yh, zh = halo
    Y, Z = g.Y, g.Z
    full = (slice(None), slice(None))
    out = []
    if pos == "first":
        out.append((0, full, None, xh[0]))
    if pos == "last":
        out.append((1, full, None, xh[1]))
    out.append((2, (slice(0, 8), slice(None)), g.row8 == 0, yh[0, pl.ds(x, 1), :]))
    out.append((3, (slice(Y - 8, Y), slice(None)), g.row8 == 7, yh[1, pl.ds(x, 1), :]))
    zlo = pltpu.roll(zh[0], lax.rem(LANES - x, LANES), 1)
    zhi = pltpu.roll(zh[1], lax.rem(LANES - 1 - x + LANES, LANES), 1)
    out.append((4, (slice(None), slice(0, LANES)), g.lane128 == 0, zlo))
    out.append((5, (slice(None), slice(Z - LANES, Z)), g.lane128 == LANES - 1, zhi))
    return out


def _masked(mask, v):
    return v if mask is None else jnp.where(mask, v, 0.0)


def _pack(g, faces, x, new, pos):
    xs, ys, zs = faces
    if pos == "first":
        xs[0] = new
    if pos == "last":
        xs[1] = new
    ys[0, pl.ds(x, 1), :] = new[0:1, :]
    ys[1, pl.ds(x, 1), :] = new[g.Y - 1 : g.Y, :]
    w0 = pltpu.roll(new[:, 0:LANES], x, 1)
    w1 = pltpu.roll(new[:, g.Z - LANES : g.Z], lax.rem(x + 1, LANES), 1)
    zs[0] = jnp.where(g.lane128 == x, w0, zs[0])
    zs[1] = jnp.where(g.lane128 == x, w1, zs[1])


def _zero_faces(faces):
    zs = faces[2]
    zs[...] = jnp.zeros(zs.shape, zs.dtype)


def _over_slabs(X, body):
    body(0, "first")
    if X > 2:

        def step(x, carry):
            body(x, "mid")
            return carry

        lax.fori_loop(1, X - 1, step, 0)
    body(X - 1, "last")


def _factor(scale, lab):
    f = jnp.where(lab == 2, scale[2], scale[3])
    f = jnp.where(lab == 1, scale[1], f)
    return jnp.where(lab == 0, scale[0], f)


def _stencil(c, nb, conds):
    total = jnp.zeros_like(c)
    for v, k in zip(nb, conds):
        total = total + k * (v - c)
    return c + HALF_RATE * total


N_EX = 2 * ITERS + 1


def _window_kernel(
    sizes,
    ckpt, diff, scale, labels, meas, obs, adj,
    grad, lam_out,
    kap, cond, u1, u2, u3, la, lb, xs, ys, zs, xh, yh, zh, send_sem, recv_sem,
):
    g = Geo(ckpt.shape)
    idx = [lax.axis_index(a) for a in AXES]

    def nbr(a, d):
        coords = list(idx)
        coords[a] = idx[a] + d
        return tuple(coords)

    def has(a, d):
        return jnp.logical_and(idx[a] + d >= 0, idx[a] + d < sizes[a])

    zs[...] = jnp.zeros(zs.shape, zs.dtype)
    halos = (xh, yh, zh)
    for a, dst in enumerate(halos):
        for s, d in ((0, -1), (1, 1)):

            @pl.when(jnp.logical_not(has(a, d)))
            def _():
                dst[:, s] = jnp.zeros(dst.shape[:1] + dst.shape[2:], dst.dtype)

    barrier = pltpu.get_barrier_semaphore()
    count = jnp.int32(0)
    for a in range(3):
        for d in (-1, 1):

            @pl.when(has(a, d))
            def _():
                pl.semaphore_signal(barrier, 1, device_id=nbr(a, d), device_id_type=MESH_ID)

            count = count + has(a, d).astype(jnp.int32)
    pl.semaphore_wait(barrier, count)

    sends = (xs, ys, zs)

    def copy(e, a, s):
        k = 2 * a + s
        return pltpu.make_async_remote_copy(
            src_ref=sends[a].at[e, 1 - s],
            dst_ref=halos[a].at[e, s],
            send_sem=send_sem.at[e, k],
            recv_sem=recv_sem.at[e, k],
            device_id=nbr(a, 1 if s == 0 else -1),
            device_id_type=MESH_ID,
        )

    def start(e):
        for a in range(3):
            for s in (0, 1):

                @pl.when(has(a, 1 if s == 0 else -1))
                def _():
                    copy(e, a, s).start()

    def wait(e):
        for a in range(3):
            for s in (0, 1):

                @pl.when(has(a, -1 if s == 0 else 1))
                def _():
                    copy(e, a, s).wait_recv()

                @pl.when(has(a, 1 if s == 0 else -1))
                def _():
                    copy(e, a, s).wait_send()

    def faces(e):
        return (xs.at[e], ys.at[e], zs.at[e])

    def halo(e):
        return (xh.at[e], yh.at[e], zh.at[e])

    def prep(x, pos):
        k = diff[x] * _factor(scale, labels[x])
        kap[x] = k
        _pack(g, faces(0), x, k, pos)
        _pack(g, faces(1), x, ckpt[x], pos)

    _over_slabs(g.X, prep)
    start(0)
    start(1)
    wait(0)

    def conduct(x, pos):
        kc, knb = _slab_nbrs(g, kap, halo(0), x, pos)
        for j, kj in enumerate(knb):
            cond[j, x] = kc + kj

    _over_slabs(g.X, conduct)

    us = (ckpt, u1, u2, u3)
    for n in range(ITERS):
        last = n == ITERS - 1
        src, out = us[n], (la if last else us[n + 1])
        e_in, e_out = 1 + n, 2 + n

        def fwd_inner(x, pos):
            c, nb = _local_nbrs(g, src, x, pos)
            out[x] = _stencil(c, nb, [cond[j, x] for j in range(6)])

        def fwd_edge(x, pos):
            for j, tile, mask, h in _edges(g, halo(e_in), x, pos):
                cc = src.at[x][tile]
                delta = _masked(mask, cond.at[j, x][tile] * (h - cc))
                out.at[x][tile] = out.at[x][tile] + HALF_RATE * delta
            new = out[x]
            if last:
                new = adj[x] + obs[x].astype(jnp.float32) * (new - meas[x])
                out[x] = new
            _pack(g, faces(e_out), x, new, pos)

        _over_slabs(g.X, fwd_inner)
        wait(e_in)
        _over_slabs(g.X, fwd_edge)
        start(e_out)

    lams = (la, lb, la, lb)
    for i, n in enumerate(range(ITERS - 1, -1, -1)):
        first, final = n == ITERS - 1, n == 0
        lam, u = lams[i], us[n]
        e_lam, e_u, e_out = ITERS + 1 + i, 1 + n, ITERS + 2 + i
        out = lam_out if final else lams[i + 1]

        def bwd_inner(x, pos):
            lc, lnb = _local_nbrs(g, lam, x, pos)
            uc, unb = _local_nbrs(g, u, x, pos)
            s = jnp.zeros_like(lc)
            t = jnp.zeros_like(lc)
            for j, (lj, uj) in enumerate(zip(lnb, unb)):
                d = lj - lc
                s = s + cond[j, x] * d
                t = t + d * (uj - uc)
            out[x] = lc + HALF_RATE * s
            term = (-HALF_RATE) * t
            grad[x] = term if first else grad[x] + term

        def bwd_edge(x, pos):
            lam_edges = _edges(g, halo(e_lam), x, pos)
            u_edges = _edges(g, halo(e_u), x, pos)
            for (j, tile, mask, hl), (_, _, _, hu) in zip(lam_edges, u_edges):
                d = hl - lam.at[x][tile]
                ds = _masked(mask, cond.at[j, x][tile] * d)
                dt = _masked(mask, d * (hu - u.at[x][tile]))
                out.at[x][tile] = out.at[x][tile] + HALF_RATE * ds
                grad.at[x][tile] = grad.at[x][tile] + (-HALF_RATE) * dt
            if final:
                grad[x] = grad[x] * _factor(scale, labels[x])
            else:
                _pack(g, faces(e_out), x, out[x], pos)

        _over_slabs(g.X, bwd_inner)
        wait(e_lam)
        _over_slabs(g.X, bwd_edge)
        if not final:
            start(e_out)


def _shards(sizes, checkpoint, diffusivity, material_scale, labels, measured, observed, adjoint_in):
    X, Y, Z = checkpoint.shape
    field = jax.ShapeDtypeStruct((X, Y, Z), jnp.float32)
    f32 = jnp.float32
    in_specs = [_vmem(), _vmem(), _smem(), _vmem(), _vmem(), _vmem(), _vmem()]
    return pl.pallas_call(
        functools.partial(_window_kernel, sizes),
        out_shape=(field, field),
        in_specs=in_specs,
        out_specs=(_vmem(), _vmem()),
        scratch_shapes=[pltpu.VMEM((X, Y, Z), f32), pltpu.VMEM((6, X, Y, Z), f32)]
        + [pltpu.VMEM((X, Y, Z), f32) for _ in range(5)]
        + [
            pltpu.VMEM((N_EX, 2, Y, Z), f32),
            pltpu.VMEM((N_EX, 2, X, Z), f32),
            pltpu.VMEM((N_EX, 2, Y, LANES), f32),
            pltpu.VMEM((N_EX, 2, Y, Z), f32),
            pltpu.VMEM((N_EX, 2, X, Z), f32),
            pltpu.VMEM((N_EX, 2, Y, LANES), f32),
            pltpu.SemaphoreType.DMA((N_EX, 6)),
            pltpu.SemaphoreType.DMA((N_EX, 6)),
        ],
        compiler_params=pltpu.CompilerParams(
            vmem_limit_bytes=VMEM_LIMIT, collective_id=0, has_side_effects=True
        ),
    )(checkpoint, diffusivity, material_scale, labels, measured, observed, adjoint_in)


def solution(mesh):
    sizes = tuple(mesh.shape[a] for a in AXES)
    block = P("gx", "gy", "gz")
    placed = (block, block, P(), block, block, block, block)
    return jax.shard_map(
        functools.partial(_shards, sizes),
        mesh=mesh,
        in_specs=placed,
        out_specs=(block, block),
        check_vma=False,
    )
```

```python
import functools

import jax
import jax.numpy as jnp
from jax import lax
from jax.experimental import pallas as pl
from jax.experimental.pallas import tpu as pltpu
from jax.sharding import PartitionSpec as P

ITERS = 4
MATERIALS = 4

RATE = 0.15
HALF_RATE = 0.5 * RATE
AXES = ("gx", "gy", "gz")
LANES = 128
VMEM_LIMIT = 56 * 1024 * 1024
MESH_ID = pl.DeviceIdType.MESH


def _vmem():
    return pl.BlockSpec(memory_space=pltpu.VMEM)


def _smem():
    return pl.BlockSpec(memory_space=pltpu.SMEM)


class Geo:
    def __init__(self, shape):
        self.X, self.Y, self.Z = shape
        self.row = lax.broadcasted_iota(jnp.int32, (self.Y, self.Z), 0)
        self.lane = lax.broadcasted_iota(jnp.int32, (self.Y, self.Z), 1)
        self.lane128 = lax.broadcasted_iota(jnp.int32, (self.Y, LANES), 1)
        self.row8 = lax.broadcasted_iota(jnp.int32, (8, self.Z), 0)

    def widen(self, v):
        return jnp.concatenate([v] * (self.Z // LANES), axis=1)


def _slab_nbrs(g, F, halo, x, pos, zl):
    xh, yh, zh = halo
    Y, Z = g.Y, g.Z
    c = F[x]
    xm = xh[0] if pos == "first" else F[x - 1]
    xp = xh[1] if pos == "last" else F[x + 1]
    ym = pltpu.roll(c, 1, 0)
    ym = jnp.concatenate([jnp.where(g.row8 == 0, yh[0, pl.ds(x, 1), :], ym[0:8]), ym[8:]], axis=0)
    yp = pltpu.roll(c, Y - 1, 0)
    yp = jnp.concatenate([yp[: Y - 8], jnp.where(g.row8 == 7, yh[1, pl.ds(x, 1), :], yp[Y - 8 :])], axis=0)
    zlo = pltpu.roll(zh[0], lax.rem(LANES - zl, LANES), 1)
    zhi = pltpu.roll(zh[1], lax.rem(LANES - 1 - zl + LANES, LANES), 1)
    zm = pltpu.roll(c, 1, 1)
    zm = jnp.concatenate([jnp.where(g.lane128 == 0, zlo, zm[:, 0:LANES]), zm[:, LANES:]], axis=1)
    zp = pltpu.roll(c, Z - 1, 1)
    zp = jnp.concatenate(
        [zp[:, : Z - LANES], jnp.where(g.lane128 == LANES - 1, zhi, zp[:, Z - LANES :])], axis=1
    )
    return c, (xm, xp, ym, yp, zm, zp)


def _pack(g, faces, x, new, pos, zl, zc):
    xs, ys = faces
    if pos == "first":
        xs[0] = new
    if pos == "last":
        xs[1] = new
    ys[0, pl.ds(x, 1), :] = new[0:1, :]
    ys[1, pl.ds(x, 1), :] = new[g.Y - 1 : g.Y, :]
    w0 = pltpu.roll(new[:, 0:LANES], zl, 1)
    w1 = pltpu.roll(new[:, g.Z - LANES : g.Z], lax.rem(zl + 1, LANES), 1)
    z0, z1 = zc
    return (jnp.where(g.lane128 == zl, w0, z0), jnp.where(g.lane128 == zl, w1, z1))


def _half(X, h, body, carry):
    H = X // 2
    if h == 0:
        if H > 1:
            carry = lax.fori_loop(1, H, lambda x, c: body(x, "mid", x, c), carry)
        return body(0, "first", 0, carry)
    if X - 1 > H:
        carry = lax.fori_loop(H, X - 1, lambda x, c: body(x, "mid", x - H, c), carry)
    return body(X - 1, "last", X - 1 - H, carry)


def _factor(scale, lab):
    f = jnp.where(lab == 2, scale[2], scale[3])
    f = jnp.where(lab == 1, scale[1], f)
    return jnp.where(lab == 0, scale[0], f)


def _stencil(c, nb, conds):
    total = jnp.zeros_like(c)
    for v, k in zip(nb, conds):
        total = total + k * (v - c)
    return c + HALF_RATE * total


N_EX = 2 * ITERS + 1
N_COPY = 10


def _window_kernel(
    sizes,
    ckpt, diff, scale, labels, meas, obs, adj,
    grad, lam_out,
    kap, cond, u1, u2, u3, la, lb, xs, ys, zs, xh, yh, zh, send_sem, recv_sem,
):
    g = Geo(ckpt.shape)
    X = g.X
    idx = [lax.axis_index(a) for a in AXES]

    def nbr(a, d):
        coords = list(idx)
        coords[a] = idx[a] + d
        return tuple(coords)

    def has(a, d):
        return jnp.logical_and(idx[a] + d >= 0, idx[a] + d < sizes[a])

    for a, dst in enumerate((xh, yh)):
        for s, d in ((0, -1), (1, 1)):

            @pl.when(jnp.logical_not(has(a, d)))
            def _():
                dst[:, s] = jnp.zeros(dst.shape[:1] + dst.shape[2:], dst.dtype)

    for s, d in ((0, -1), (1, 1)):

        @pl.when(jnp.logical_not(has(2, d)))
        def _():
            zh[:, :, s] = jnp.zeros(zh.shape[:2] + zh.shape[3:], zh.dtype)

    barrier = pltpu.get_barrier_semaphore()
    count = jnp.int32(0)
    for a in range(3):
        for d in (-1, 1):

            @pl.when(has(a, d))
            def _():
                pl.semaphore_signal(barrier, 1, device_id=nbr(a, d), device_id_type=MESH_ID)

            count = count + has(a, d).astype(jnp.int32)
    pl.semaphore_wait(barrier, count)

    H = X // 2

    def copy(e, k):
        if k < 2:
            a, s, src, dst = 0, k, xs.at[e, 1 - k], xh.at[e, k]
        elif k < 6:
            h, s = divmod(k - 2, 2)
            rows = pl.ds(h * H, H) if h == 0 else pl.ds(H, X - H)
            a, src, dst = 1, ys.at[e, 1 - s, rows], yh.at[e, s, rows]
        else:
            h, s = divmod(k - 6, 2)
            a, src, dst = 2, zs.at[e, h, 1 - s], zh.at[e, h, s]
        d = 1 if s == 0 else -1
        desc = pltpu.make_async_remote_copy(
            src_ref=src,
            dst_ref=dst,
            send_sem=send_sem.at[e, k],
            recv_sem=recv_sem.at[e, k],
            device_id=nbr(a, d),
            device_id_type=MESH_ID,
        )
        return desc, a, d

    def start(e, ks):
        for k in ks:
            desc, a, d = copy(e, k)

            @pl.when(has(a, d))
            def _():
                desc.start()

    def wait_recv(e, ks):
        for k in ks:
            desc, a, d = copy(e, k)

            @pl.when(has(a, -d))
            def _():
                desc.wait_recv()

    def wait_send(e, ks):
        for k in ks:
            desc, a, d = copy(e, k)

            @pl.when(has(a, d))
            def _():
                desc.wait_send()

    SENT = ((1, 2, 3, 6, 7), (0, 4, 5, 8, 9))
    NEED = ((2, 3, 6, 7), (1, 4, 5, 8, 9))

    def faces(e):
        return (xs.at[e], ys.at[e])

    def halo(e, h):
        return (xh.at[e], yh.at[e], zh.at[e, h])

    def zero_z():
        z = jnp.zeros((g.Y, LANES), jnp.float32)
        return (z, z)

    def store_z(e, h, zc):
        zs[e, h, 0] = zc[0]
        zs[e, h, 1] = zc[1]

    def sweep(e_in, e_out, body):
        for h in (0, 1):
            if e_in is not None:
                wait_recv(e_in, NEED[h])
                if h == 1:
                    wait_send(e_in, range(N_COPY))

            def run(x, pos, zl, zc):
                if pos == "first" and e_in is not None:
                    wait_recv(e_in, (0,))
                return body(x, pos, zl, zc, h)

            zc = _half(X, h, run, zero_z())
            if e_out is not None:
                store_z(e_out, h, zc)
                start(e_out, SENT[h])

    def prep(x, pos, zl, zc, h):
        k = diff[x] * _factor(scale, labels[x])
        kap[x] = k
        zk, zu = zc
        zk = _pack(g, faces(0), x, k, pos, zl, zk)
        zu = _pack(g, faces(1), x, ckpt[x], pos, zl, zu)
        return (zk, zu)

    for h in (0, 1):
        zc = _half(X, h, lambda x, pos, zl, zc: prep(x, pos, zl, zc, h), (zero_z(), zero_z()))
        store_z(0, h, zc[0])
        store_z(1, h, zc[1])
        start(0, SENT[h])
        start(1, SENT[h])

    def conduct(x, pos, zl, zc, h):
        kc, knb = _slab_nbrs(g, kap, halo(0, h), x, pos, zl)
        for j, kj in enumerate(knb):
            cond[j, x] = kc + kj
        return zc

    sweep(0, None, conduct)

    us = (ckpt, u1, u2, u3)
    for n in range(ITERS):
        last = n == ITERS - 1
        src, out = us[n], (la if last else us[n + 1])
        e_in, e_out = 1 + n, 2 + n

        def fwd(x, pos, zl, zc, h):
            c, nb = _slab_nbrs(g, src, halo(e_in, h), x, pos, zl)
            new = _stencil(c, nb, [cond[j, x] for j in range(6)])
            if last:
                new = adj[x] + obs[x].astype(jnp.float32) * (new - meas[x])
            out[x] = new
            return _pack(g, faces(e_out), x, new, pos, zl, zc)

        sweep(e_in, e_out, fwd)

    lams = (la, lb, la, lb)
    for i, n in enumerate(range(ITERS - 1, -1, -1)):
        first, final = n == ITERS - 1, n == 0
        lam, u = lams[i], us[n]
        e_lam, e_u, e_out = ITERS + 1 + i, 1 + n, ITERS + 2 + i
        out = lam_out if final else lams[i + 1]

        def bwd(x, pos, zl, zc, h):
            lc, lnb = _slab_nbrs(g, lam, halo(e_lam, h), x, pos, zl)
            uc, unb = _slab_nbrs(g, u, halo(e_u, h), x, pos, zl)
            s = jnp.zeros_like(lc)
            t = jnp.zeros_like(lc)
            for j, (lj, uj) in enumerate(zip(lnb, unb)):
                d = lj - lc
                s = s + cond[j, x] * d
                t = t + d * (uj - uc)
            new = lc + HALF_RATE * s
            term = (-HALF_RATE) * t
            acc = term if first else grad[x] + term
            if final:
                acc = acc * _factor(scale, labels[x])
            grad[x] = acc
            out[x] = new
            if final:
                return zc
            return _pack(g, faces(e_out), x, new, pos, zl, zc)

        sweep(e_lam, None if final else e_out, bwd)


def _shards(sizes, checkpoint, diffusivity, material_scale, labels, measured, observed, adjoint_in):
    X, Y, Z = checkpoint.shape
    field = jax.ShapeDtypeStruct((X, Y, Z), jnp.float32)
    f32 = jnp.float32
    in_specs = [_vmem(), _vmem(), _smem(), _vmem(), _vmem(), _vmem(), _vmem()]
    return pl.pallas_call(
        functools.partial(_window_kernel, sizes),
        out_shape=(field, field),
        in_specs=in_specs,
        out_specs=(_vmem(), _vmem()),
        scratch_shapes=[pltpu.VMEM((X, Y, Z), f32), pltpu.VMEM((6, X, Y, Z), f32)]
        + [pltpu.VMEM((X, Y, Z), f32) for _ in range(5)]
        + [
            pltpu.VMEM((N_EX, 2, Y, Z), f32),
            pltpu.VMEM((N_EX, 2, X, Z), f32),
            pltpu.VMEM((N_EX, 2, 2, Y, LANES), f32),
            pltpu.VMEM((N_EX, 2, Y, Z), f32),
            pltpu.VMEM((N_EX, 2, X, Z), f32),
            pltpu.VMEM((N_EX, 2, 2, Y, LANES), f32),
            pltpu.SemaphoreType.DMA((N_EX, N_COPY)),
            pltpu.SemaphoreType.DMA((N_EX, N_COPY)),
        ],
        compiler_params=pltpu.CompilerParams(
            vmem_limit_bytes=VMEM_LIMIT, collective_id=0, has_side_effects=True
        ),
    )(checkpoint, diffusivity, material_scale, labels, measured, observed, adjoint_in)


def solution(mesh):
    sizes = tuple(mesh.shape[a] for a in AXES)
    block = P("gx", "gy", "gz")
    placed = (block, block, P(), block, block, block, block)
    return jax.shard_map(
        functools.partial(_shards, sizes),
        mesh=mesh,
        in_specs=placed,
        out_specs=(block, block),
        check_vma=False,
    )
```

```python
import functools

import jax
import jax.numpy as jnp
from jax import lax
from jax.experimental import pallas as pl
from jax.experimental.pallas import tpu as pltpu
from jax.sharding import PartitionSpec as P

ITERS = 4
MATERIALS = 4

RATE = 0.15
HALF_RATE = 0.5 * RATE
AXES = ("gx", "gy", "gz")
LANES = 128
VMEM_LIMIT = 56 * 1024 * 1024
MESH_ID = pl.DeviceIdType.MESH


def _vmem():
    return pl.BlockSpec(memory_space=pltpu.VMEM)


def _smem():
    return pl.BlockSpec(memory_space=pltpu.SMEM)


class Geo:
    def __init__(self, shape):
        self.X, self.Y, self.Z = shape
        self.row = lax.broadcasted_iota(jnp.int32, (self.Y, self.Z), 0)
        self.lane = lax.broadcasted_iota(jnp.int32, (self.Y, self.Z), 1)
        self.lane128 = lax.broadcasted_iota(jnp.int32, (self.Y, LANES), 1)
        self.row8 = lax.broadcasted_iota(jnp.int32, (8, self.Z), 0)

    def widen(self, v):
        return jnp.concatenate([v] * (self.Z // LANES), axis=1)


def _slab_nbrs(g, F, halo, x, pos, zl):
    xh, yh, zh = halo
    Y, Z = g.Y, g.Z
    c = F[x]
    xm = xh[0] if pos == "first" else F[x - 1]
    xp = xh[1] if pos == "last" else F[x + 1]
    ym = pltpu.roll(c, 1, 0)
    ym = jnp.concatenate([jnp.where(g.row8 == 0, yh[0, pl.ds(x, 1), :], ym[0:8]), ym[8:]], axis=0)
    yp = pltpu.roll(c, Y - 1, 0)
    yp = jnp.concatenate([yp[: Y - 8], jnp.where(g.row8 == 7, yh[1, pl.ds(x, 1), :], yp[Y - 8 :])], axis=0)
    zlo = pltpu.roll(zh[0], lax.rem(LANES - zl, LANES), 1)
    zhi = pltpu.roll(zh[1], lax.rem(LANES - 1 - zl + LANES, LANES), 1)
    zm = pltpu.roll(c, 1, 1)
    zm = jnp.concatenate([jnp.where(g.lane128 == 0, zlo, zm[:, 0:LANES]), zm[:, LANES:]], axis=1)
    zp = pltpu.roll(c, Z - 1, 1)
    zp = jnp.concatenate(
        [zp[:, : Z - LANES], jnp.where(g.lane128 == LANES - 1, zhi, zp[:, Z - LANES :])], axis=1
    )
    return c, (xm, xp, ym, yp, zm, zp)


def _pack(g, faces, x, new, pos, zl, zc):
    xs, ys = faces
    if pos == "first":
        xs[0] = new
    if pos == "last":
        xs[1] = new
    ys[0, pl.ds(x, 1), :] = new[0:1, :]
    ys[1, pl.ds(x, 1), :] = new[g.Y - 1 : g.Y, :]
    w0 = pltpu.roll(new[:, 0:LANES], zl, 1)
    w1 = pltpu.roll(new[:, g.Z - LANES : g.Z], lax.rem(zl + 1, LANES), 1)
    z0, z1 = zc
    return (jnp.where(g.lane128 == zl, w0, z0), jnp.where(g.lane128 == zl, w1, z1))


def _half(X, h, body, carry):
    H = X // 2
    if h == 0:
        if H > 1:
            carry = lax.fori_loop(1, H, lambda x, c: body(x, "mid", x, c), carry)
        return body(0, "first", 0, carry)
    if X - 1 > H:
        carry = lax.fori_loop(H, X - 1, lambda x, c: body(x, "mid", x - H, c), carry)
    return body(X - 1, "last", X - 1 - H, carry)


def _factor(scale, lab):
    f = jnp.where(lab == 2, scale[2], scale[3])
    f = jnp.where(lab == 1, scale[1], f)
    return jnp.where(lab == 0, scale[0], f)


def _stencil(c, nb, conds):
    total = jnp.zeros_like(c)
    for v, k in zip(nb, conds):
        total = total + k * (v - c)
    return c + HALF_RATE * total


N_EX = 2 * ITERS + 1
N_COPY = 10


def _window_kernel(
    sizes,
    ckpt_hbm, diff_hbm, scale, labels_hbm, meas_hbm, obs_hbm, adj_hbm,
    grad, lam_out,
    ckpt, diff, labels, meas, obs, adj,
    kap, cond, u1, u2, u3, la, lb, xs, ys, zs, xh, yh, zh, send_sem, recv_sem, load_sem,
):
    g = Geo(ckpt.shape)
    X = g.X
    H = X // 2
    halves = (pl.ds(0, H), pl.ds(H, X - H))
    early = ((ckpt_hbm, ckpt), (diff_hbm, diff), (labels_hbm, labels))
    late = ((meas_hbm, meas), (obs_hbm, obs), (adj_hbm, adj))

    def load(i, src, dst, rows=None):
        if rows is not None:
            src, dst = src.at[rows], dst.at[rows]
        return pltpu.make_async_copy(src, dst, load_sem.at[i])

    def early_load(h, i):
        src, dst = early[i]
        return load(2 * i + h, src, dst, halves[h])

    for h in (0, 1):
        for i in range(3):
            early_load(h, i).start()
    for i, (src, dst) in enumerate(late):
        load(6 + i, src, dst).start()
    idx = [lax.axis_index(a) for a in AXES]

    def nbr(a, d):
        coords = list(idx)
        coords[a] = idx[a] + d
        return tuple(coords)

    def has(a, d):
        return jnp.logical_and(idx[a] + d >= 0, idx[a] + d < sizes[a])

    for a, dst in enumerate((xh, yh)):
        for s, d in ((0, -1), (1, 1)):

            @pl.when(jnp.logical_not(has(a, d)))
            def _():
                dst[:, s] = jnp.zeros(dst.shape[:1] + dst.shape[2:], dst.dtype)

    for s, d in ((0, -1), (1, 1)):

        @pl.when(jnp.logical_not(has(2, d)))
        def _():
            zh[:, :, s] = jnp.zeros(zh.shape[:2] + zh.shape[3:], zh.dtype)

    barrier = pltpu.get_barrier_semaphore()
    count = jnp.int32(0)
    for a in range(3):
        for d in (-1, 1):

            @pl.when(has(a, d))
            def _():
                pl.semaphore_signal(barrier, 1, device_id=nbr(a, d), device_id_type=MESH_ID)

            count = count + has(a, d).astype(jnp.int32)
    pl.semaphore_wait(barrier, count)

    def copy(e, k):
        if k < 2:
            a, s, src, dst = 0, k, xs.at[e, 1 - k], xh.at[e, k]
        elif k < 6:
            h, s = divmod(k - 2, 2)
            rows = pl.ds(h * H, H) if h == 0 else pl.ds(H, X - H)
            a, src, dst = 1, ys.at[e, 1 - s, rows], yh.at[e, s, rows]
        else:
            h, s = divmod(k - 6, 2)
            a, src, dst = 2, zs.at[e, h, 1 - s], zh.at[e, h, s]
        d = 1 if s == 0 else -1
        desc = pltpu.make_async_remote_copy(
            src_ref=src,
            dst_ref=dst,
            send_sem=send_sem.at[e, k],
            recv_sem=recv_sem.at[e, k],
            device_id=nbr(a, d),
            device_id_type=MESH_ID,
        )
        return desc, a, d

    def start(e, ks):
        for k in ks:
            desc, a, d = copy(e, k)

            @pl.when(has(a, d))
            def _():
                desc.start()

    def wait_recv(e, ks):
        for k in ks:
            desc, a, d = copy(e, k)

            @pl.when(has(a, -d))
            def _():
                desc.wait_recv()

    def wait_send(e, ks):
        for k in ks:
            desc, a, d = copy(e, k)

            @pl.when(has(a, d))
            def _():
                desc.wait_send()

    SENT = ((1, 2, 3, 6, 7), (0, 4, 5, 8, 9))
    NEED = ((2, 3, 6, 7), (1, 4, 5, 8, 9))

    def faces(e):
        return (xs.at[e], ys.at[e])

    def halo(e, h):
        return (xh.at[e], yh.at[e], zh.at[e, h])

    def zero_z():
        z = jnp.zeros((g.Y, LANES), jnp.float32)
        return (z, z)

    def store_z(e, h, zc):
        zs[e, h, 0] = zc[0]
        zs[e, h, 1] = zc[1]

    def sweep(e_in, e_out, body):
        for h in (0, 1):
            if e_in is not None:
                wait_recv(e_in, NEED[h])
                if h == 1:
                    wait_send(e_in, range(N_COPY))

            def run(x, pos, zl, zc):
                if pos == "first" and e_in is not None:
                    wait_recv(e_in, (0,))
                return body(x, pos, zl, zc, h)

            zc = _half(X, h, run, zero_z())
            if e_out is not None:
                store_z(e_out, h, zc)
                start(e_out, SENT[h])

    def prep(x, pos, zl, zc, h):
        k = diff[x] * _factor(scale, labels[x])
        kap[x] = k
        zk, zu = zc
        zk = _pack(g, faces(0), x, k, pos, zl, zk)
        zu = _pack(g, faces(1), x, ckpt[x], pos, zl, zu)
        return (zk, zu)

    for h in (0, 1):
        for i in range(3):
            early_load(h, i).wait()
        zc = _half(X, h, lambda x, pos, zl, zc: prep(x, pos, zl, zc, h), (zero_z(), zero_z()))
        store_z(0, h, zc[0])
        store_z(1, h, zc[1])
        start(0, SENT[h])
        start(1, SENT[h])

    def conduct(x, pos, zl, zc, h):
        kc, knb = _slab_nbrs(g, kap, halo(0, h), x, pos, zl)
        for j, kj in enumerate(knb):
            cond[j, x] = kc + kj
        return zc

    sweep(0, None, conduct)

    us = (ckpt, u1, u2, u3)
    for n in range(ITERS):
        last = n == ITERS - 1
        src, out = us[n], (la if last else us[n + 1])
        e_in, e_out = 1 + n, 2 + n
        if last:
            for i, (src_hbm, dst) in enumerate(late):
                load(6 + i, src_hbm, dst).wait()

        def fwd(x, pos, zl, zc, h):
            c, nb = _slab_nbrs(g, src, halo(e_in, h), x, pos, zl)
            new = _stencil(c, nb, [cond[j, x] for j in range(6)])
            if last:
                new = adj[x] + obs[x].astype(jnp.float32) * (new - meas[x])
            out[x] = new
            return _pack(g, faces(e_out), x, new, pos, zl, zc)

        sweep(e_in, e_out, fwd)

    lams = (la, lb, la, lb)
    for i, n in enumerate(range(ITERS - 1, -1, -1)):
        first, final = n == ITERS - 1, n == 0
        lam, u = lams[i], us[n]
        e_lam, e_u, e_out = ITERS + 1 + i, 1 + n, ITERS + 2 + i
        out = lam_out if final else lams[i + 1]

        def bwd(x, pos, zl, zc, h):
            lc, lnb = _slab_nbrs(g, lam, halo(e_lam, h), x, pos, zl)
            uc, unb = _slab_nbrs(g, u, halo(e_u, h), x, pos, zl)
            s = jnp.zeros_like(lc)
            t = jnp.zeros_like(lc)
            for j, (lj, uj) in enumerate(zip(lnb, unb)):
                d = lj - lc
                s = s + cond[j, x] * d
                t = t + d * (uj - uc)
            new = lc + HALF_RATE * s
            term = (-HALF_RATE) * t
            acc = term if first else grad[x] + term
            if final:
                acc = acc * _factor(scale, labels[x])
            grad[x] = acc
            out[x] = new
            if final:
                return zc
            return _pack(g, faces(e_out), x, new, pos, zl, zc)

        sweep(e_lam, None if final else e_out, bwd)


def _shards(sizes, checkpoint, diffusivity, material_scale, labels, measured, observed, adjoint_in):
    X, Y, Z = checkpoint.shape
    field = jax.ShapeDtypeStruct((X, Y, Z), jnp.float32)
    f32 = jnp.float32
    hbm = pl.BlockSpec(memory_space=pl.ANY)
    in_specs = [hbm, hbm, _smem(), hbm, hbm, hbm, hbm]
    i32 = jnp.int32
    return pl.pallas_call(
        functools.partial(_window_kernel, sizes),
        out_shape=(field, field),
        in_specs=in_specs,
        out_specs=(_vmem(), _vmem()),
        scratch_shapes=[pltpu.VMEM((X, Y, Z), t) for t in (f32, f32, i32, f32, i32, f32)]
        + [pltpu.VMEM((X, Y, Z), f32), pltpu.VMEM((6, X, Y, Z), f32)]
        + [pltpu.VMEM((X, Y, Z), f32) for _ in range(5)]
        + [
            pltpu.VMEM((N_EX, 2, Y, Z), f32),
            pltpu.VMEM((N_EX, 2, X, Z), f32),
            pltpu.VMEM((N_EX, 2, 2, Y, LANES), f32),
            pltpu.VMEM((N_EX, 2, Y, Z), f32),
            pltpu.VMEM((N_EX, 2, X, Z), f32),
            pltpu.VMEM((N_EX, 2, 2, Y, LANES), f32),
            pltpu.SemaphoreType.DMA((N_EX, N_COPY)),
            pltpu.SemaphoreType.DMA((N_EX, N_COPY)),
            pltpu.SemaphoreType.DMA((9,)),
        ],
        compiler_params=pltpu.CompilerParams(
            vmem_limit_bytes=VMEM_LIMIT, collective_id=0, has_side_effects=True
        ),
    )(checkpoint, diffusivity, material_scale, labels, measured, observed, adjoint_in)


def solution(mesh):
    sizes = tuple(mesh.shape[a] for a in AXES)
    block = P("gx", "gy", "gz")
    placed = (block, block, P(), block, block, block, block)
    return jax.shard_map(
        functools.partial(_shards, sizes),
        mesh=mesh,
        in_specs=placed,
        out_specs=(block, block),
        check_vma=False,
    )
```

```python
import functools

import jax
import jax.numpy as jnp
from jax import lax
from jax.experimental import pallas as pl
from jax.experimental.pallas import tpu as pltpu
from jax.sharding import PartitionSpec as P

ITERS = 4
MATERIALS = 4

RATE = 0.15
HALF_RATE = 0.5 * RATE
AXES = ("gx", "gy", "gz")
LANES = 128
VMEM_LIMIT = 56 * 1024 * 1024
MESH_ID = pl.DeviceIdType.MESH


def _vmem():
    return pl.BlockSpec(memory_space=pltpu.VMEM)


def _smem():
    return pl.BlockSpec(memory_space=pltpu.SMEM)


class Geo:
    def __init__(self, shape):
        self.X, self.Y, self.Z = shape
        self.row = lax.broadcasted_iota(jnp.int32, (self.Y, self.Z), 0)
        self.lane = lax.broadcasted_iota(jnp.int32, (self.Y, self.Z), 1)
        self.lane128 = lax.broadcasted_iota(jnp.int32, (self.Y, LANES), 1)
        self.row8 = lax.broadcasted_iota(jnp.int32, (8, self.Z), 0)

    def widen(self, v):
        return jnp.concatenate([v] * (self.Z // LANES), axis=1)


def _slab_nbrs(g, F, halo, x, pos, zl):
    xh, yh, zh = halo
    Y, Z = g.Y, g.Z
    c = F[x]
    xm = xh[0] if pos == "first" else F[x - 1]
    xp = xh[1] if pos == "last" else F[x + 1]
    ym = pltpu.roll(c, 1, 0)
    ym = jnp.concatenate([jnp.where(g.row8 == 0, yh[0, pl.ds(zl, 1), :], ym[0:8]), ym[8:]], axis=0)
    yp = pltpu.roll(c, Y - 1, 0)
    yp = jnp.concatenate([yp[: Y - 8], jnp.where(g.row8 == 7, yh[1, pl.ds(zl, 1), :], yp[Y - 8 :])], axis=0)
    zlo = pltpu.roll(zh[0], lax.rem(LANES - zl, LANES), 1)
    zhi = pltpu.roll(zh[1], lax.rem(LANES - 1 - zl + LANES, LANES), 1)
    zm = pltpu.roll(c, 1, 1)
    zm = jnp.concatenate([jnp.where(g.lane128 == 0, zlo, zm[:, 0:LANES]), zm[:, LANES:]], axis=1)
    zp = pltpu.roll(c, Z - 1, 1)
    zp = jnp.concatenate(
        [zp[:, : Z - LANES], jnp.where(g.lane128 == LANES - 1, zhi, zp[:, Z - LANES :])], axis=1
    )
    return c, (xm, xp, ym, yp, zm, zp)


def _pack(g, faces, x, new, pos, zl, zc):
    xs, ys = faces
    if pos == "first":
        xs[0] = new
    if pos == "last":
        xs[1] = new
    ys[0, pl.ds(zl, 1), :] = new[0:1, :]
    ys[1, pl.ds(zl, 1), :] = new[g.Y - 1 : g.Y, :]
    w0 = pltpu.roll(new[:, 0:LANES], zl, 1)
    w1 = pltpu.roll(new[:, g.Z - LANES : g.Z], lax.rem(zl + 1, LANES), 1)
    z0, z1 = zc
    return (jnp.where(g.lane128 == zl, w0, z0), jnp.where(g.lane128 == zl, w1, z1))


def _groups(X):
    H = X // 2
    return ((None, 2), (1, H - 1), (H, X - 1 - H))


def _group(X, gi, body, carry):
    if gi == 0:
        carry = body(0, "first", 0, carry)
        return body(X - 1, "last", 1, carry)
    x0, n = _groups(X)[gi]
    if n > 0:
        carry = lax.fori_loop(x0, x0 + n, lambda x, c: body(x, "mid", x - x0, c), carry)
    return carry


def _factor(scale, lab):
    f = jnp.where(lab == 2, scale[2], scale[3])
    f = jnp.where(lab == 1, scale[1], f)
    return jnp.where(lab == 0, scale[0], f)


def _stencil(c, nb, conds):
    total = jnp.zeros_like(c)
    for v, k in zip(nb, conds):
        total = total + k * (v - c)
    return c + HALF_RATE * total


N_EX = 2 * ITERS + 1
N_COPY = 14


def _window_kernel(
    sizes,
    ckpt_hbm, diff_hbm, scale, labels_hbm, meas_hbm, obs_hbm, adj_hbm,
    grad, lam_out,
    ckpt, diff, labels, meas, obs, adj,
    kap, cond, u1, u2, u3, la, lb, xs, ys, zs, xh, yh, zh, send_sem, recv_sem, load_sem,
):
    g = Geo(ckpt.shape)
    X = g.X
    chunks = (pl.ds(0, 1), pl.ds(X - 1, 1)) + tuple(pl.ds(x0, n) for x0, n in _groups(X)[1:] if n > 0)
    n_chunk = len(chunks)
    early = ((ckpt_hbm, ckpt), (diff_hbm, diff), (labels_hbm, labels))
    late = ((meas_hbm, meas), (obs_hbm, obs), (adj_hbm, adj))

    def load(i, src, dst, rows=None):
        if rows is not None:
            src, dst = src.at[rows], dst.at[rows]
        return pltpu.make_async_copy(src, dst, load_sem.at[i])

    def early_load(c, i):
        src, dst = early[i]
        return load(n_chunk * i + c, src, dst, chunks[c])

    def group_chunks(gi):
        if gi == 0:
            return (0, 1)
        return tuple(c for c in range(2, n_chunk) if c - 1 == gi)

    for c in range(n_chunk):
        for i in range(3):
            early_load(c, i).start()
    for i, (src, dst) in enumerate(late):
        load(3 * n_chunk + i, src, dst).start()

    idx = [lax.axis_index(a) for a in AXES]

    def nbr(a, d):
        coords = list(idx)
        coords[a] = idx[a] + d
        return tuple(coords)

    def has(a, d):
        return jnp.logical_and(idx[a] + d >= 0, idx[a] + d < sizes[a])

    for s, d in ((0, -1), (1, 1)):

        @pl.when(jnp.logical_not(has(0, d)))
        def _():
            xh[:, s] = jnp.zeros(xh.shape[:1] + xh.shape[2:], xh.dtype)

        for a, dst in ((1, yh), (2, zh)):

            @pl.when(jnp.logical_not(has(a, d)))
            def _():
                dst[:, :, s] = jnp.zeros(dst.shape[:2] + dst.shape[3:], dst.dtype)

    barrier = pltpu.get_barrier_semaphore()
    count = jnp.int32(0)
    for a in range(3):
        for d in (-1, 1):

            @pl.when(has(a, d))
            def _():
                pl.semaphore_signal(barrier, 1, device_id=nbr(a, d), device_id_type=MESH_ID)

            count = count + has(a, d).astype(jnp.int32)
    pl.semaphore_wait(barrier, count)

    def copy(e, k):
        if k < 2:
            a, s, src, dst = 0, k, xs.at[e, 1 - k], xh.at[e, k]
        else:
            gi, r = divmod(k - 2, 4)
            kind, s = divmod(r, 2)
            a = 1 + kind
            buf_s, buf_h = (ys, yh) if kind == 0 else (zs, zh)
            src, dst = buf_s.at[e, gi, 1 - s], buf_h.at[e, gi, s]
        d = 1 if s == 0 else -1
        desc = pltpu.make_async_remote_copy(
            src_ref=src,
            dst_ref=dst,
            send_sem=send_sem.at[e, k],
            recv_sem=recv_sem.at[e, k],
            device_id=nbr(a, d),
            device_id_type=MESH_ID,
        )
        return desc, a, d

    def start(e, ks):
        for k in ks:
            desc, a, d = copy(e, k)

            @pl.when(has(a, d))
            def _():
                desc.start()

    def wait_recv(e, ks):
        for k in ks:
            desc, a, d = copy(e, k)

            @pl.when(has(a, -d))
            def _():
                desc.wait_recv()

    def wait_send(e, ks):
        for k in ks:
            desc, a, d = copy(e, k)

            @pl.when(has(a, d))
            def _():
                desc.wait_send()

    def group_copies(gi):
        return tuple(2 + 4 * gi + r for r in range(4)) + ((0, 1) if gi == 0 else ())

    def faces(e, gi):
        return (xs.at[e], ys.at[e, gi])

    def halo(e, gi):
        return (xh.at[e], yh.at[e, gi], zh.at[e, gi])

    def zero_z():
        z = jnp.zeros((g.Y, LANES), jnp.float32)
        return (z, z)

    def store_z(e, gi, zc):
        zs[e, gi, 0] = zc[0]
        zs[e, gi, 1] = zc[1]

    def sweep(e_in, e_out, body):
        for gi in range(3):
            if e_in is not None:
                wait_recv(e_in, group_copies(gi))
            zc = _group(X, gi, lambda x, pos, zl, zc: body(x, pos, zl, zc, gi), zero_z())
            if e_out is not None:
                store_z(e_out, gi, zc)
                start(e_out, group_copies(gi))
        if e_in is not None:
            wait_send(e_in, range(N_COPY))

    def prep(x, pos, zl, zc, gi):
        k = diff[x] * _factor(scale, labels[x])
        kap[x] = k
        zk, zu = zc
        zk = _pack(g, faces(0, gi), x, k, pos, zl, zk)
        zu = _pack(g, faces(1, gi), x, ckpt[x], pos, zl, zu)
        return (zk, zu)

    for gi in range(3):
        for c in group_chunks(gi):
            for i in range(3):
                early_load(c, i).wait()
        zc = _group(X, gi, lambda x, pos, zl, zc: prep(x, pos, zl, zc, gi), (zero_z(), zero_z()))
        store_z(0, gi, zc[0])
        store_z(1, gi, zc[1])
        start(0, group_copies(gi))
        start(1, group_copies(gi))

    def conduct(x, pos, zl, zc, h):
        kc, knb = _slab_nbrs(g, kap, halo(0, h), x, pos, zl)
        for j, kj in enumerate(knb):
            cond[j, x] = kc + kj
        return zc

    sweep(0, None, conduct)

    us = (ckpt, u1, u2, u3)
    for n in range(ITERS):
        last = n == ITERS - 1
        src, out = us[n], (la if last else us[n + 1])
        e_in, e_out = 1 + n, 2 + n
        if last:
            for i, (src_hbm, dst) in enumerate(late):
                load(3 * n_chunk + i, src_hbm, dst).wait()

        def fwd(x, pos, zl, zc, h):
            c, nb = _slab_nbrs(g, src, halo(e_in, h), x, pos, zl)
            new = _stencil(c, nb, [cond[j, x] for j in range(6)])
            if last:
                new = adj[x] + obs[x].astype(jnp.float32) * (new - meas[x])
            out[x] = new
            return _pack(g, faces(e_out, h), x, new, pos, zl, zc)

        sweep(e_in, e_out, fwd)

    lams = (la, lb, la, lb)
    for i, n in enumerate(range(ITERS - 1, -1, -1)):
        first, final = n == ITERS - 1, n == 0
        lam, u = lams[i], us[n]
        e_lam, e_u, e_out = ITERS + 1 + i, 1 + n, ITERS + 2 + i
        out = lam_out if final else lams[i + 1]

        def bwd(x, pos, zl, zc, h):
            lc, lnb = _slab_nbrs(g, lam, halo(e_lam, h), x, pos, zl)
            uc, unb = _slab_nbrs(g, u, halo(e_u, h), x, pos, zl)
            s = jnp.zeros_like(lc)
            t = jnp.zeros_like(lc)
            for j, (lj, uj) in enumerate(zip(lnb, unb)):
                d = lj - lc
                s = s + cond[j, x] * d
                t = t + d * (uj - uc)
            new = lc + HALF_RATE * s
            term = (-HALF_RATE) * t
            acc = term if first else grad[x] + term
            if final:
                acc = acc * _factor(scale, labels[x])
            grad[x] = acc
            out[x] = new
            if final:
                return zc
            return _pack(g, faces(e_out, h), x, new, pos, zl, zc)

        sweep(e_lam, None if final else e_out, bwd)


def _shards(sizes, checkpoint, diffusivity, material_scale, labels, measured, observed, adjoint_in):
    X, Y, Z = checkpoint.shape
    field = jax.ShapeDtypeStruct((X, Y, Z), jnp.float32)
    f32 = jnp.float32
    rows = -(-max(n for _, n in _groups(X)) // 8) * 8
    hbm = pl.BlockSpec(memory_space=pl.ANY)
    in_specs = [hbm, hbm, _smem(), hbm, hbm, hbm, hbm]
    i32 = jnp.int32
    return pl.pallas_call(
        functools.partial(_window_kernel, sizes),
        out_shape=(field, field),
        in_specs=in_specs,
        out_specs=(_vmem(), _vmem()),
        scratch_shapes=[pltpu.VMEM((X, Y, Z), t) for t in (f32, f32, i32, f32, i32, f32)]
        + [pltpu.VMEM((X, Y, Z), f32), pltpu.VMEM((6, X, Y, Z), f32)]
        + [pltpu.VMEM((X, Y, Z), f32) for _ in range(5)]
        + [
            pltpu.VMEM((N_EX, 2, Y, Z), f32),
            pltpu.VMEM((N_EX, 3, 2, rows, Z), f32),
            pltpu.VMEM((N_EX, 3, 2, Y, LANES), f32),
            pltpu.VMEM((N_EX, 2, Y, Z), f32),
            pltpu.VMEM((N_EX, 3, 2, rows, Z), f32),
            pltpu.VMEM((N_EX, 3, 2, Y, LANES), f32),
            pltpu.SemaphoreType.DMA((N_EX, N_COPY)),
            pltpu.SemaphoreType.DMA((N_EX, N_COPY)),
            pltpu.SemaphoreType.DMA((3 * 4 + 3,)),
        ],
        compiler_params=pltpu.CompilerParams(
            vmem_limit_bytes=VMEM_LIMIT, collective_id=0, has_side_effects=True
        ),
    )(checkpoint, diffusivity, material_scale, labels, measured, observed, adjoint_in)


def solution(mesh):
    sizes = tuple(mesh.shape[a] for a in AXES)
    block = P("gx", "gy", "gz")
    placed = (block, block, P(), block, block, block, block)
    return jax.shard_map(
        functools.partial(_shards, sizes),
        mesh=mesh,
        in_specs=placed,
        out_specs=(block, block),
        check_vma=False,
    )
```

```python
import functools

import jax
import jax.numpy as jnp
from jax import lax
from jax.experimental import pallas as pl
from jax.experimental.pallas import tpu as pltpu
from jax.sharding import PartitionSpec as P

ITERS = 4
MATERIALS = 4

RATE = 0.15
HALF_RATE = 0.5 * RATE
AXES = ("gx", "gy", "gz")
LANES = 128
VMEM_LIMIT = 56 * 1024 * 1024
MESH_ID = pl.DeviceIdType.MESH


def _vmem():
    return pl.BlockSpec(memory_space=pltpu.VMEM)


def _smem():
    return pl.BlockSpec(memory_space=pltpu.SMEM)


class Geo:
    def __init__(self, shape):
        self.X, self.Y, self.Z = shape
        self.row = lax.broadcasted_iota(jnp.int32, (self.Y, self.Z), 0)
        self.lane = lax.broadcasted_iota(jnp.int32, (self.Y, self.Z), 1)
        self.lane128 = lax.broadcasted_iota(jnp.int32, (self.Y, LANES), 1)
        self.row8 = lax.broadcasted_iota(jnp.int32, (8, self.Z), 0)

    def widen(self, v):
        return jnp.concatenate([v] * (self.Z // LANES), axis=1)


def _slab_nbrs(g, F, halo, x, pos, zl):
    xh, yh, zh = halo
    Y, Z = g.Y, g.Z
    c = F[x]
    xm = xh[0] if pos == "first" else F[x - 1]
    xp = xh[1] if pos == "last" else F[x + 1]
    ym = pltpu.roll(c, 1, 0)
    ym = jnp.concatenate([jnp.where(g.row8 == 0, yh[0, pl.ds(zl, 1), :], ym[0:8]), ym[8:]], axis=0)
    yp = pltpu.roll(c, Y - 1, 0)
    yp = jnp.concatenate([yp[: Y - 8], jnp.where(g.row8 == 7, yh[1, pl.ds(zl, 1), :], yp[Y - 8 :])], axis=0)
    zlo = pltpu.roll(zh[0], lax.rem(LANES - zl, LANES), 1)
    zhi = pltpu.roll(zh[1], lax.rem(LANES - 1 - zl + LANES, LANES), 1)
    zm = pltpu.roll(c, 1, 1)
    zm = jnp.concatenate([jnp.where(g.lane128 == 0, zlo, zm[:, 0:LANES]), zm[:, LANES:]], axis=1)
    zp = pltpu.roll(c, Z - 1, 1)
    zp = jnp.concatenate(
        [zp[:, : Z - LANES], jnp.where(g.lane128 == LANES - 1, zhi, zp[:, Z - LANES :])], axis=1
    )
    return c, (xm, xp, ym, yp, zm, zp)


def _pack(g, faces, x, new, pos, zl, zc):
    xs, ys = faces
    if pos == "first":
        xs[0] = new
    if pos == "last":
        xs[1] = new
    ys[0, pl.ds(zl, 1), :] = new[0:1, :]
    ys[1, pl.ds(zl, 1), :] = new[g.Y - 1 : g.Y, :]
    w0 = pltpu.roll(new[:, 0:LANES], zl, 1)
    w1 = pltpu.roll(new[:, g.Z - LANES : g.Z], lax.rem(zl + 1, LANES), 1)
    z0, z1 = zc
    return (jnp.where(g.lane128 == zl, w0, z0), jnp.where(g.lane128 == zl, w1, z1))


def _groups(X):
    H = X // 2
    return ((None, 2), (1, H - 1), (H, X - 1 - H))


def _group(X, gi, body, carry):
    if gi == 0:
        carry = body(0, "first", 0, carry)
        return body(X - 1, "last", 1, carry)
    x0, n = _groups(X)[gi]
    if n > 0:
        carry = lax.fori_loop(x0, x0 + n, lambda x, c: body(x, "mid", x - x0, c), carry)
    return carry


def _factor(scale, lab):
    f = jnp.where(lab == 2, scale[2], scale[3])
    f = jnp.where(lab == 1, scale[1], f)
    return jnp.where(lab == 0, scale[0], f)


def _stencil(c, nb, conds):
    total = jnp.zeros_like(c)
    for v, k in zip(nb, conds):
        total = total + k * (v - c)
    return c + HALF_RATE * total


N_EX = 2 * ITERS + 1
N_COPY = 14


def _window_kernel(
    sizes,
    ckpt_hbm, diff_hbm, scale, labels_hbm, meas_hbm, obs_hbm, adj_hbm,
    grad, lam_out,
    ckpt, diff, labels, meas, obs, adj,
    kap, cond, u1, u2, u3, la, lb, xs, ys, zs, xh, yh, zh, send_sem, recv_sem, load_sem,
):
    g = Geo(ckpt.shape)
    X = g.X
    chunks = (pl.ds(0, 1), pl.ds(X - 1, 1)) + tuple(pl.ds(x0, n) for x0, n in _groups(X)[1:] if n > 0)
    n_chunk = len(chunks)
    early = ((ckpt_hbm, ckpt), (diff_hbm, diff), (labels_hbm, labels))
    late = ((meas_hbm, meas), (obs_hbm, obs), (adj_hbm, adj))

    def load(i, src, dst, rows=None):
        if rows is not None:
            src, dst = src.at[rows], dst.at[rows]
        return pltpu.make_async_copy(src, dst, load_sem.at[i])

    def early_load(c, i):
        src, dst = early[i]
        return load(n_chunk * i + c, src, dst, chunks[c])

    def group_chunks(gi):
        if gi == 0:
            return (0, 1)
        return tuple(c for c in range(2, n_chunk) if c - 1 == gi)

    for c in range(n_chunk):
        for i in range(3):
            early_load(c, i).start()
    for i, (src, dst) in enumerate(late):
        load(3 * n_chunk + i, src, dst).start()

    idx = [lax.axis_index(a) for a in AXES]

    def nbr(a, d):
        coords = list(idx)
        coords[a] = idx[a] + d
        return tuple(coords)

    def has(a, d):
        return jnp.logical_and(idx[a] + d >= 0, idx[a] + d < sizes[a])

    for s, d in ((0, -1), (1, 1)):

        @pl.when(jnp.logical_not(has(0, d)))
        def _():
            xh[:, s] = jnp.zeros(xh.shape[:1] + xh.shape[2:], xh.dtype)

        for a, dst in ((1, yh), (2, zh)):

            @pl.when(jnp.logical_not(has(a, d)))
            def _():
                dst[:, :, s] = jnp.zeros(dst.shape[:2] + dst.shape[3:], dst.dtype)

    barrier = pltpu.get_barrier_semaphore()
    count = jnp.int32(0)
    for a in range(3):
        for d in (-1, 1):

            @pl.when(has(a, d))
            def _():
                pl.semaphore_signal(barrier, 1, device_id=nbr(a, d), device_id_type=MESH_ID)

            count = count + has(a, d).astype(jnp.int32)
    pl.semaphore_wait(barrier, count)

    def copy(e, k):
        if k < 2:
            a, s, src, dst = 0, k, xs.at[e, 1 - k], xh.at[e, k]
        else:
            gi, r = divmod(k - 2, 4)
            kind, s = divmod(r, 2)
            a = 1 + kind
            buf_s, buf_h = (ys, yh) if kind == 0 else (zs, zh)
            src, dst = buf_s.at[e, gi, 1 - s], buf_h.at[e, gi, s]
        d = 1 if s == 0 else -1
        desc = pltpu.make_async_remote_copy(
            src_ref=src,
            dst_ref=dst,
            send_sem=send_sem.at[e, k],
            recv_sem=recv_sem.at[e, k],
            device_id=nbr(a, d),
            device_id_type=MESH_ID,
        )
        return desc, a, d

    def start(e, ks):
        for k in ks:
            desc, a, d = copy(e, k)

            @pl.when(has(a, d))
            def _():
                desc.start()

    def wait_recv(e, ks):
        for k in ks:
            desc, a, d = copy(e, k)

            @pl.when(has(a, -d))
            def _():
                desc.wait_recv()

    def wait_send(e, ks):
        for k in ks:
            desc, a, d = copy(e, k)

            @pl.when(has(a, d))
            def _():
                desc.wait_send()

    def group_copies(gi):
        return ((0, 1) if gi == 0 else ()) + tuple(2 + 4 * gi + r for r in range(4))

    def faces(e, gi):
        return (xs.at[e], ys.at[e, gi])

    def halo(e, gi):
        return (xh.at[e], yh.at[e, gi], zh.at[e, gi])

    def zero_z():
        z = jnp.zeros((g.Y, LANES), jnp.float32)
        return (z, z)

    def store_z(e, gi, zc):
        zs[e, gi, 0] = zc[0]
        zs[e, gi, 1] = zc[1]

    def sweep(e_in, e_out, body):
        for gi in range(3):
            if e_in is not None:
                wait_recv(e_in, group_copies(gi))
            zc = _group(X, gi, lambda x, pos, zl, zc: body(x, pos, zl, zc, gi), zero_z())
            if e_out is not None:
                store_z(e_out, gi, zc)
                start(e_out, group_copies(gi))
        if e_in is not None:
            wait_send(e_in, range(N_COPY))

    def prep(x, pos, zl, zc, gi):
        k = diff[x] * _factor(scale, labels[x])
        kap[x] = k
        zk, zu = zc
        zk = _pack(g, faces(0, gi), x, k, pos, zl, zk)
        zu = _pack(g, faces(1, gi), x, ckpt[x], pos, zl, zu)
        return (zk, zu)

    for gi in range(3):
        for c in group_chunks(gi):
            for i in range(3):
                early_load(c, i).wait()
        zc = _group(X, gi, lambda x, pos, zl, zc: prep(x, pos, zl, zc, gi), (zero_z(), zero_z()))
        store_z(0, gi, zc[0])
        store_z(1, gi, zc[1])
        start(0, group_copies(gi))
        start(1, group_copies(gi))

    def conduct(x, pos, zl, zc, h):
        kc, knb = _slab_nbrs(g, kap, halo(0, h), x, pos, zl)
        for j, kj in enumerate(knb):
            cond[j, x] = kc + kj
        return zc

    sweep(0, None, conduct)

    us = (ckpt, u1, u2, u3)
    for n in range(ITERS):
        last = n == ITERS - 1
        src, out = us[n], (la if last else us[n + 1])
        e_in, e_out = 1 + n, 2 + n
        if last:
            for i, (src_hbm, dst) in enumerate(late):
                load(3 * n_chunk + i, src_hbm, dst).wait()

        def fwd(x, pos, zl, zc, h):
            c, nb = _slab_nbrs(g, src, halo(e_in, h), x, pos, zl)
            new = _stencil(c, nb, [cond[j, x] for j in range(6)])
            if last:
                new = adj[x] + obs[x].astype(jnp.float32) * (new - meas[x])
            out[x] = new
            return _pack(g, faces(e_out, h), x, new, pos, zl, zc)

        sweep(e_in, e_out, fwd)

    lams = (la, lb, la, lb)
    for i, n in enumerate(range(ITERS - 1, -1, -1)):
        first, final = n == ITERS - 1, n == 0
        lam, u = lams[i], us[n]
        e_lam, e_u, e_out = ITERS + 1 + i, 1 + n, ITERS + 2 + i
        out = lam_out if final else lams[i + 1]

        def bwd(x, pos, zl, zc, h):
            lc, lnb = _slab_nbrs(g, lam, halo(e_lam, h), x, pos, zl)
            uc, unb = _slab_nbrs(g, u, halo(e_u, h), x, pos, zl)
            s = jnp.zeros_like(lc)
            t = jnp.zeros_like(lc)
            for j, (lj, uj) in enumerate(zip(lnb, unb)):
                d = lj - lc
                s = s + cond[j, x] * d
                t = t + d * (uj - uc)
            new = lc + HALF_RATE * s
            term = (-HALF_RATE) * t
            acc = term if first else grad[x] + term
            if final:
                acc = acc * _factor(scale, labels[x])
            grad[x] = acc
            out[x] = new
            if final:
                return zc
            return _pack(g, faces(e_out, h), x, new, pos, zl, zc)

        sweep(e_lam, None if final else e_out, bwd)


def _shards(sizes, checkpoint, diffusivity, material_scale, labels, measured, observed, adjoint_in):
    X, Y, Z = checkpoint.shape
    field = jax.ShapeDtypeStruct((X, Y, Z), jnp.float32)
    f32 = jnp.float32
    rows = -(-max(n for _, n in _groups(X)) // 8) * 8
    hbm = pl.BlockSpec(memory_space=pl.ANY)
    in_specs = [hbm, hbm, _smem(), hbm, hbm, hbm, hbm]
    i32 = jnp.int32
    return pl.pallas_call(
        functools.partial(_window_kernel, sizes),
        out_shape=(field, field),
        in_specs=in_specs,
        out_specs=(_vmem(), _vmem()),
        scratch_shapes=[pltpu.VMEM((X, Y, Z), t) for t in (f32, f32, i32, f32, i32, f32)]
        + [pltpu.VMEM((X, Y, Z), f32), pltpu.VMEM((6, X, Y, Z), f32)]
        + [pltpu.VMEM((X, Y, Z), f32) for _ in range(5)]
        + [
            pltpu.VMEM((N_EX, 2, Y, Z), f32),
            pltpu.VMEM((N_EX, 3, 2, rows, Z), f32),
            pltpu.VMEM((N_EX, 3, 2, Y, LANES), f32),
            pltpu.VMEM((N_EX, 2, Y, Z), f32),
            pltpu.VMEM((N_EX, 3, 2, rows, Z), f32),
            pltpu.VMEM((N_EX, 3, 2, Y, LANES), f32),
            pltpu.SemaphoreType.DMA((N_EX, N_COPY)),
            pltpu.SemaphoreType.DMA((N_EX, N_COPY)),
            pltpu.SemaphoreType.DMA((3 * 4 + 3,)),
        ],
        compiler_params=pltpu.CompilerParams(
            vmem_limit_bytes=VMEM_LIMIT, collective_id=0, has_side_effects=True
        ),
    )(checkpoint, diffusivity, material_scale, labels, measured, observed, adjoint_in)


def solution(mesh):
    sizes = tuple(mesh.shape[a] for a in AXES)
    block = P("gx", "gy", "gz")
    placed = (block, block, P(), block, block, block, block)
    return jax.shard_map(
        functools.partial(_shards, sizes),
        mesh=mesh,
        in_specs=placed,
        out_specs=(block, block),
        check_vma=False,
    )
```
